32 devices in a mesh: grp: 2 (over x), tok: 16 (over z, y, core).
Axes of the slice: x: 2, y: 2, z: 4, core: 2. Of those that a mesh axis runs over, the one named last changes fastest.
Arguments:
- tokens: bfloat16 [4096, 2048], P(('grp', 'tok')), parts along dimension 0, may hold values from -6 to 6
- norm_gain: float32 [2048], replicated, may hold values from 0.1 to 1.9
- expert_ids: int32 [4096, 8], P(('grp', 'tok')), parts along dimension 0, may hold values from 0 to 15, as said below
- gate_weights: float32 [4096, 8], P(('grp', 'tok')), parts along dimension 0, may hold values from 0.05 to 1
- owner_map: int32 [16], replicated, may hold values from 0 to 15, each once
- in_q: bfloat16 [16, 2, 2048, 768], P('tok'), may hold values from -0.125 to 0.125
- in_scale: bfloat16 [16, 2, 768], P('tok'), may hold values from 0.5 to 2
- down_q: bfloat16 [16, 768, 2048], P('tok'), may hold values from -0.21875 to 0.21875
- down_scale: bfloat16 [16, 2048], P('tok'), may hold values from 0.5 to 2
Outputs:
- moe_out: bfloat16 [4096, 2048], P(('grp', 'tok')), parts along dimension 0
The draws below stay inside these ranges and needn't reach their ends.
There are 2 independent parts, one for each index of `grp`. The reference program is written for one: setup_inputs(seed, part) draws one part's arguments, and reference() takes and returns one part's arrays. A program takes and returns all parts, laid end to end along the dimension named above; an argument that names none is the same for every part. Nothing has to cross between parts.
Inputs may be any that keep to these rules, and one draw needn't show every extreme that they name: `expert_ids`: each row names 8 different experts. One and the same expert is named by exactly 96 of the 128 rows of every device; every other expert is named by between 32 and 80 rows of each device, and 80 is reached on every device. `owner_map`: every slot holds exactly one expert.
All inputs are finite; a program needn't handle non-finite values.
Results may differ from the reference program's by a relative error of at most 0.0071.
Values may be sent and summed in bfloat16 or wider, within the bound.
No kernel may reach another device: no remote copies, remote signals or barrier semaphores. Data moves between devices by JAX's collectives and lax.ppermute only.
A program may use at most 128 MiB of HBM per device.

```python
import math
import jax
import jax.numpy as jnp
from jax import lax

D = 2048
FF = 768
TOP = 8
TOK_DEV = 128
EXPERTS = 16
TOKENS = 2048
MOST = 96
N_TOK = 16


def block_routes(block_key, hot_expert):
    mean_load = TOK_DEV * TOP // EXPERTS
    spread = mean_load // 4
    pair_count = (EXPERTS - 2) // 2
    key_order, key_amount, key_rows, key_columns = jax.random.split(block_key, 4)
    labels = jnp.arange(EXPERTS, dtype=jnp.int32)
    shuffled = jax.random.permutation(key_order, EXPERTS).astype(jnp.int32)
    ranking = jnp.where(labels == hot_expert, -1, shuffled)
    expert_order = jnp.argsort(ranking).astype(jnp.int32)
    amounts = jax.random.randint(key_amount, (pair_count,), 0, spread + 1).astype(jnp.int32)
    amounts = amounts.at[0].set(spread)
    head = jnp.full((1,), mean_load + mean_load // 2, jnp.int32)
    tail = jnp.full((1,), mean_load - mean_load // 2, jnp.int32)
    load_counts = jnp.concatenate([head, mean_load + amounts, mean_load - amounts, tail])
    load_ends = jnp.cumsum(load_counts).astype(jnp.int32)
    position = jnp.arange(TOK_DEV * TOP, dtype=jnp.int32)
    group_index = jnp.searchsorted(load_ends, position, side='right').astype(jnp.int32)
    listed = expert_order[group_index]
    table_grid = listed.reshape(TOP, TOK_DEV).T
    table_grid = table_grid[jax.random.permutation(key_rows, TOK_DEV)]
    column_noise = jax.random.randint(key_columns, (TOK_DEV, TOP), 0, 1 << 20).astype(jnp.int32) * TOP
    column_noise = column_noise + jnp.arange(TOP, dtype=jnp.int32)
    column_order = jnp.argsort(column_noise, axis=1)
    return jnp.take_along_axis(table_grid, column_order, axis=1)


def draw_expert_ids(key, part):
    base_key = jax.random.fold_in(key, 17)
    key_hot, key_blocks = jax.random.split(base_key)
    hot_expert = jax.random.randint(key_hot, (), 0, EXPERTS).astype(jnp.int32)
    block_keys = jax.random.split(key_blocks, TOKENS // TOK_DEV)
    routes = jax.vmap(block_routes, in_axes=(0, None))(block_keys, hot_expert)
    return routes.reshape(TOKENS, TOP).astype(jnp.int32)


def levels(key, shape, shards, low, top_value):
    def one(dim, parts):
        heights = jax.random.uniform(jax.random.fold_in(jax.random.fold_in(key, 6), dim), (parts,), jnp.float32, low / len(shards), top_value / len(shards))
        return jnp.repeat(jnp.exp(heights), shape[dim] // parts).reshape((-1,) + (1,) * (len(shape) - dim - 1))

    level = one(*shards[0])
    for cut in shards[1:]:
        level = level * one(*cut)
    return level


def centred(key, shape, width, reach, cuts=(), held_as=jnp.bfloat16):
    factor_of = levels(key, shape, cuts, -0.22, 0.18) if cuts else 1.0
    values = jax.random.normal(key, shape, jnp.float32) * width * factor_of
    return jnp.minimum(jnp.maximum(values, -reach), reach).astype(held_as)


def setup_inputs(seed: int = 0, part: int = 0) -> dict:
    arg_keys = jax.random.split(jax.random.key(seed), 10)
    part_keys = jax.random.split(jax.random.fold_in(arg_keys[9], part), 10)
    tokens = centred(part_keys[0], (TOKENS, D), 1.0, 6.0, ((0, 16),))
    norm_gain = jnp.clip(1.0 + 0.18 * jax.random.normal(arg_keys[1], (D,), jnp.float32), 0.1, 1.9)
    expert_ids = draw_expert_ids(jax.random.fold_in(jax.random.fold_in(arg_keys[9], part), 71), part)
    gate_weights = jnp.clip(jnp.exp(math.log(1.0) - 2.9957323 * jax.random.uniform(part_keys[3], (TOKENS, TOP), jnp.float32) ** levels(part_keys[3], (TOKENS, TOP), ((0, 16),), -0.2, 0.2)), 0.05, 1.0)
    owner_map = jax.random.permutation(arg_keys[4], EXPERTS).astype(jnp.int32)
    in_q = centred(arg_keys[5], (EXPERTS, 2, D, FF), D ** -0.5, 0.125, ((0, 16),))
    in_scale = jnp.clip(jnp.exp(math.log(2.0) - 1.3862944 * jax.random.uniform(arg_keys[6], (EXPERTS, 2, FF), jnp.float32) ** levels(arg_keys[6], (EXPERTS, 2, FF), ((0, 16),), -0.2, 0.2)), 0.5, 2.0).astype(jnp.bfloat16)
    down_q = centred(arg_keys[7], (EXPERTS, FF, D), FF ** -0.5, 0.21875, ((0, 16),))
    down_scale = jnp.clip(jnp.exp(math.log(2.0) - 1.3862944 * jax.random.uniform(arg_keys[8], (EXPERTS, D), jnp.float32) ** levels(arg_keys[8], (EXPERTS, D), ((0, 16),), -0.2, 0.2)), 0.5, 2.0).astype(jnp.bfloat16)
    return dict(tokens=tokens, norm_gain=norm_gain, expert_ids=expert_ids, gate_weights=gate_weights, owner_map=owner_map, in_q=in_q, in_scale=in_scale, down_q=down_q, down_scale=down_scale)


def expert_rows(batch_rows, in_blocks, in_scales, down_block, down_scales):
    gate_part = jnp.dot(batch_rows, in_blocks[0], preferred_element_type=jnp.float32) * in_scales[0]
    up_part = jnp.dot(batch_rows, in_blocks[1], preferred_element_type=jnp.float32) * in_scales[1]
    hidden = (jax.nn.silu(gate_part) * up_part).astype(jnp.bfloat16)
    return (jnp.dot(hidden, down_block, preferred_element_type=jnp.float32) * down_scales).astype(jnp.bfloat16)

def reference(tokens, norm_gain, expert_ids, gate_weights, owner_map, in_q, in_scale, down_q, down_scale):
    values = tokens.astype(jnp.float32)
    row_scale = lax.rsqrt(lax.optimization_barrier(jnp.mean(values * values, axis=1, keepdims=True)) + 1e-06)
    normed = (values * row_scale * norm_gain).astype(jnp.bfloat16)
    weights = gate_weights / lax.optimization_barrier(jnp.sum(gate_weights, axis=1, keepdims=True))
    flat_slot = owner_map[expert_ids].reshape(-1).astype(jnp.int32)
    flat_weight = weights.reshape(-1)
    assigned = TOKENS * TOP
    limit = N_TOK * MOST
    padded_rows = jnp.concatenate([normed, jnp.zeros((1, D), jnp.bfloat16)], axis=0)
    padded_weight = jnp.concatenate([flat_weight, jnp.zeros((1,), jnp.float32)], axis=0)

    def visit(total, pack):
        slot_id, in_blocks, in_scales, down_block, down_scales = pack
        chosen = jnp.nonzero(flat_slot == slot_id, size=limit, fill_value=assigned)[0].astype(jnp.int32)
        token_index = (chosen // TOP).astype(jnp.int32)
        served = expert_rows(padded_rows[token_index], in_blocks, in_scales, down_block, down_scales)
        share = padded_weight[chosen][:, None] * served.astype(jnp.float32)
        return (total.at[token_index].add(share), None)
    start_total = jnp.zeros((TOKENS + 1, D), jnp.float32)
    slot_ids = jnp.arange(EXPERTS, dtype=jnp.int32)
    total, unused = lax.scan(visit, start_total, (slot_ids, in_q, in_scale, down_q, down_scale))
    return total[:TOKENS].astype(jnp.bfloat16)
```

```python
import jax
import jax.numpy as jnp
from jax import lax
from jax.sharding import PartitionSpec as P


def expert_rows(batch_rows, in_blocks, in_scales, down_block, down_scales):
    gate_part = jnp.dot(batch_rows, in_blocks[0], preferred_element_type=jnp.float32) * in_scales[0]
    up_part = jnp.dot(batch_rows, in_blocks[1], preferred_element_type=jnp.float32) * in_scales[1]
    hidden = (jax.nn.silu(gate_part) * up_part).astype(jnp.bfloat16)
    return jnp.dot(hidden, down_block, preferred_element_type=jnp.float32) * down_scales


def normalized(tokens, norm_gain):
    values = tokens.astype(jnp.float32)
    row_scale = lax.rsqrt(jnp.mean(values * values, axis=1, keepdims=True) + 1e-06)
    return (values * row_scale * norm_gain).astype(jnp.bfloat16)


def exchanged(
    tokens, norm_gain, expert_ids, gate_weights, owner_map, in_q, in_scale, down_q, down_scale
):
    tok_rows, model_width = tokens.shape
    top_count = expert_ids.shape[1]
    experts = owner_map.shape[0]
    mean_load = tok_rows * top_count // experts
    capacity = mean_load + mean_load // 2
    normed = normalized(tokens, norm_gain)
    weights = gate_weights / jnp.sum(gate_weights, axis=1, keepdims=True)
    labels = jnp.arange(experts, dtype=jnp.int32)
    slot_table = jnp.sum(jnp.where(expert_ids[:, :, None] == labels, owner_map, 0), axis=2)
    flat_slot = slot_table.reshape(-1)
    onehot = (flat_slot[:, None] == labels).astype(jnp.int32)
    slot_rank = jnp.sum((jnp.cumsum(onehot, axis=0) - onehot) * onehot, axis=1)
    repeated = jnp.repeat(normed, top_count, axis=0)
    outgoing = (
        jnp.zeros((experts, capacity, model_width), jnp.bfloat16)
        .at[flat_slot, slot_rank]
        .set(repeated)
    )
    received = lax.all_to_all(outgoing, "tok", split_axis=0, concat_axis=0, tiled=True)
    source_count, slot_count, unused_width = received.shape
    flat_rows = received.reshape(source_count * slot_count, model_width)
    served = expert_rows(flat_rows, in_q[0], in_scale[0], down_q[0], down_scale[0])
    served = served.astype(jnp.bfloat16).reshape(source_count, slot_count, model_width)
    returned_rows = lax.all_to_all(served, "tok", split_axis=0, concat_axis=0, tiled=True)
    picked = returned_rows[flat_slot, slot_rank].reshape(tok_rows, top_count, model_width)
    mixed = jnp.sum(weights[:, :, None] * picked.astype(jnp.float32), axis=1)
    return mixed.astype(jnp.bfloat16)


def ring_pairs(devices):
    chips = devices // 2
    loop = list(range(0, chips, 2)) + list(range(chips - 1, 0, -2))
    pairs = []
    for place, chip in enumerate(loop):
        after = loop[(place + 1) % chips]
        pairs.append((2 * chip, 2 * after))
        pairs.append((2 * after + 1, 2 * chip + 1))
    return pairs, chips


def circulated(
    tokens, norm_gain, expert_ids, gate_weights, owner_map, in_q, in_scale, down_q, down_scale
):
    tok_rows, model_width = tokens.shape
    experts = owner_map.shape[0]
    devices = lax.axis_size("tok")
    ring, chips = ring_pairs(devices)
    swap = [(i, i ^ 1) for i in range(devices)]
    me = lax.axis_index("tok")
    lanes = -(-2 * experts // 128) * 128
    labels = jnp.arange(experts, dtype=jnp.int32)
    my_expert = jnp.sum(jnp.where(owner_map == me, labels, 0))

    normed = normalized(tokens, norm_gain)
    weights = gate_weights / jnp.sum(gate_weights, axis=1, keepdims=True)
    named = expert_ids[:, :, None] == labels
    table = jnp.sum(jnp.where(named, weights[:, :, None], 0.0), axis=1)
    high = lax.reduce_precision(table, 8, 7)
    low = table - high
    fill = jnp.zeros((tok_rows, lanes - 2 * experts), jnp.float32)
    extra = jnp.concatenate([high, low, fill], axis=1).astype(jnp.bfloat16)
    block = jnp.concatenate([normed, extra], axis=1)
    lane = jnp.arange(lanes, dtype=jnp.int32)
    mine = (lane == my_expert) | (lane == my_expert + experts)

    def served(rows):
        share = jnp.sum(jnp.where(mine, rows[:, model_width:].astype(jnp.float32), 0.0), axis=1)
        out = expert_rows(rows[:, :model_width], in_q[0], in_scale[0], down_q[0], down_scale[0])
        return out * share[:, None]

    total = None
    for step in range(chips):
        other = lax.ppermute(block, "tok", swap)
        both = served(jnp.concatenate([block, other], axis=0))
        if step < chips - 1:
            block = lax.ppermute(block, "tok", ring)
        lent = lax.ppermute(both[tok_rows:].astype(jnp.bfloat16), "tok", swap)
        part = both[:tok_rows] + lent.astype(jnp.float32)
        if step == 0:
            own = part
            continue
        if total is not None:
            part = part + total.astype(jnp.float32)
        total = lax.ppermute(part.astype(jnp.bfloat16), "tok", ring)
    return (own + total.astype(jnp.float32)).astype(jnp.bfloat16)


def solution(mesh):
    def on_device(tokens, norm_gain, expert_ids, gate_weights, owner_map, *blocks):
        tok_rows, experts = tokens.shape[0], owner_map.shape[0]
        mean_load = tok_rows * expert_ids.shape[1] // experts
        routed = experts * (mean_load + mean_load // 2)
        dense = tok_rows * mesh.shape["tok"]
        form = circulated if dense <= 2 * routed and mesh.shape["tok"] % 4 == 0 else exchanged
        return form(tokens, norm_gain, expert_ids, gate_weights, owner_map, *blocks)

    in_specs = (
        P(("grp", "tok"), None),
        P(),
        P(("grp", "tok"), None),
        P(("grp", "tok"), None),
        P(),
        P("tok", None, None, None),
        P("tok", None, None),
        P("tok", None, None),
        P("tok", None),
    )
    out_specs = P(("grp", "tok"), None)
    return jax.shard_map(
        on_device, mesh=mesh, in_specs=in_specs, out_specs=out_specs, check_vma=False
    )
```

```python
import functools

import jax
import jax.numpy as jnp
from jax import lax
from jax.experimental import pallas as pl
from jax.experimental.pallas import tpu as pltpu
from jax.sharding import PartitionSpec as P

TILE = 256
SMALL = 8 << 20
LARGE = 20 << 20


def expert_rows(batch_rows, in_blocks, in_scales, down_block, down_scales):
    gate_part = jnp.dot(batch_rows, in_blocks[0], preferred_element_type=jnp.float32) * in_scales[0]
    up_part = jnp.dot(batch_rows, in_blocks[1], preferred_element_type=jnp.float32) * in_scales[1]
    hidden = (jax.nn.silu(gate_part) * up_part).astype(jnp.bfloat16)
    return jnp.dot(hidden, down_block, preferred_element_type=jnp.float32) * down_scales


def normalized(tokens, norm_gain):
    values = tokens.astype(jnp.float32)
    row_scale = lax.rsqrt(jnp.mean(values * values, axis=1, keepdims=True) + 1e-06)
    return (values * row_scale * norm_gain).astype(jnp.bfloat16)


def exchanged(
    tokens, norm_gain, expert_ids, gate_weights, owner_map, in_q, in_scale, down_q, down_scale
):
    tok_rows, model_width = tokens.shape
    top_count = expert_ids.shape[1]
    experts = owner_map.shape[0]
    mean_load = tok_rows * top_count // experts
    capacity = mean_load + mean_load // 2
    normed = normalized(tokens, norm_gain)
    weights = gate_weights / jnp.sum(gate_weights, axis=1, keepdims=True)
    labels = jnp.arange(experts, dtype=jnp.int32)
    slot_table = jnp.sum(jnp.where(expert_ids[:, :, None] == labels, owner_map, 0), axis=2)
    flat_slot = slot_table.reshape(-1)
    onehot = (flat_slot[:, None] == labels).astype(jnp.int32)
    slot_rank = jnp.sum((jnp.cumsum(onehot, axis=0) - onehot) * onehot, axis=1)
    repeated = jnp.repeat(normed, top_count, axis=0)
    outgoing = (
        jnp.zeros((experts, capacity, model_width), jnp.bfloat16)
        .at[flat_slot, slot_rank]
        .set(repeated)
    )
    received = lax.all_to_all(outgoing, "tok", split_axis=0, concat_axis=0, tiled=True)
    source_count, slot_count, unused_width = received.shape
    flat_rows = received.reshape(source_count * slot_count, model_width)
    served = expert_rows(flat_rows, in_q[0], in_scale[0], down_q[0], down_scale[0])
    served = served.astype(jnp.bfloat16).reshape(source_count, slot_count, model_width)
    returned_rows = lax.all_to_all(served, "tok", split_axis=0, concat_axis=0, tiled=True)
    picked = returned_rows[flat_slot, slot_rank].reshape(tok_rows, top_count, model_width)
    mixed = jnp.sum(weights[:, :, None] * picked.astype(jnp.float32), axis=1)
    return mixed.astype(jnp.bfloat16)


def ring_pairs(devices):
    chips = devices // 2
    loop = list(range(0, chips, 2)) + list(range(chips - 1, 0, -2))
    pairs = []
    for place, chip in enumerate(loop):
        after = loop[(place + 1) % chips]
        pairs.append((2 * chip, 2 * after))
        pairs.append((2 * after + 1, 2 * chip + 1))
    return pairs, chips


def packed_kernel(experts, tokens_ref, gain_ref, ids_ref, gates_ref, out_ref):
    tok_rows, model_width = tokens_ref.shape
    values = tokens_ref[...].astype(jnp.float32)
    row_scale = lax.rsqrt(jnp.mean(values * values, axis=1, keepdims=True) + 1e-06)
    out_ref[:, :model_width] = (values * row_scale * gain_ref[...]).astype(jnp.bfloat16)
    gates = gates_ref[...]
    weights = gates / jnp.sum(gates, axis=1, keepdims=True)
    lanes = out_ref.shape[1] - model_width
    lane = lax.broadcasted_iota(jnp.int32, (tok_rows, lanes), 1)
    label = jnp.where(lane < experts, lane, lane - experts)
    table = jnp.zeros((tok_rows, lanes), jnp.float32)
    for k in range(ids_ref.shape[1]):
        table += jnp.where(label == ids_ref[:, k : k + 1], weights[:, k : k + 1], 0.0)
    high = table.astype(jnp.bfloat16).astype(jnp.float32)
    out_ref[:, model_width:] = jnp.where(lane < experts, high, table - high).astype(jnp.bfloat16)


def packed(tokens, norm_gain, expert_ids, gate_weights, experts):
    tok_rows, model_width = tokens.shape
    lanes = -(-2 * experts // 128) * 128
    return pl.pallas_call(
        functools.partial(packed_kernel, experts),
        out_shape=jax.ShapeDtypeStruct((tok_rows, model_width + lanes), jnp.bfloat16),
        in_specs=[pl.BlockSpec(memory_space=pltpu.VMEM)] * 4,
        out_specs=pl.BlockSpec(memory_space=pltpu.VMEM),
        compiler_params=pltpu.CompilerParams(vmem_limit_bytes=SMALL),
        name="packed",
    )(tokens, norm_gain[None, :], expert_ids, gate_weights)


def visit_kernel(
    experts, mine_ref, near_ref, far_ref, in_ref, in_scale_ref, down_ref, down_scale_ref,
    part_ref, lent_ref, rows_ref, hidden_ref,
):
    tok_rows, model_width = part_ref.shape
    hidden_width = hidden_ref.shape[1]
    rows_ref[:tok_rows] = near_ref[:, :model_width]
    rows_ref[tok_rows:] = far_ref[:, :model_width]
    rows = rows_ref[...]
    for start in range(0, hidden_width, TILE):
        cols = slice(start, start + TILE)
        gate = jnp.dot(rows, in_ref[0, 0, :, cols], preferred_element_type=jnp.float32)
        up = jnp.dot(rows, in_ref[0, 1, :, cols], preferred_element_type=jnp.float32)
        gate = gate * in_scale_ref[0, 0:1, cols].astype(jnp.float32)
        up = up * in_scale_ref[0, 1:2, cols].astype(jnp.float32)
        hidden_ref[:, cols] = (gate / (1.0 + jnp.exp(-gate)) * up).astype(jnp.bfloat16)
    lane = lax.broadcasted_iota(jnp.int32, (tok_rows, far_ref.shape[1] - model_width), 1)
    chosen = (lane == mine_ref[0]) | (lane == mine_ref[0] + experts)
    near = near_ref[:, model_width:].astype(jnp.float32)
    far = far_ref[:, model_width:].astype(jnp.float32)
    near_share = jnp.sum(jnp.where(chosen, near, 0.0), axis=1, keepdims=True)
    far_share = jnp.sum(jnp.where(chosen, far, 0.0), axis=1, keepdims=True)
    hidden = hidden_ref[...]
    for start in range(0, model_width, TILE):
        cols = slice(start, start + TILE)
        out = jnp.dot(hidden, down_ref[0, :, cols], preferred_element_type=jnp.float32)
        out = out * down_scale_ref[:, cols].astype(jnp.float32)
        part_ref[:, cols] = out[:tok_rows] * near_share
        lent_ref[:, cols] = (out[tok_rows:] * far_share).astype(jnp.bfloat16)


def visit(my_expert, near, far, experts, in_q, in_scale, down_q, down_scale):
    tok_rows = near.shape[0]
    hidden_width, model_width = down_q.shape[1:]
    flops = 2 * 2 * tok_rows * 3 * hidden_width * model_width
    return pl.pallas_call(
        functools.partial(visit_kernel, experts),
        out_shape=(
            jax.ShapeDtypeStruct((tok_rows, model_width), jnp.float32),
            jax.ShapeDtypeStruct((tok_rows, model_width), jnp.bfloat16),
        ),
        in_specs=[pl.BlockSpec(memory_space=pltpu.SMEM)]
        + [pl.BlockSpec(memory_space=pltpu.VMEM)] * 6,
        out_specs=(pl.BlockSpec(memory_space=pltpu.VMEM),) * 2,
        scratch_shapes=[
            pltpu.VMEM((2 * tok_rows, model_width), jnp.bfloat16),
            pltpu.VMEM((2 * tok_rows, hidden_width), jnp.bfloat16),
        ],
        compiler_params=pltpu.CompilerParams(vmem_limit_bytes=LARGE),
        cost_estimate=pl.CostEstimate(
            flops=flops, bytes_accessed=6 * tok_rows * model_width, transcendentals=0
        ),
        name="visit",
    )(my_expert, near, far, in_q, in_scale, down_q, down_scale)


def circulated(
    tokens, norm_gain, expert_ids, gate_weights, owner_map, in_q, in_scale, down_q, down_scale
):
    experts = owner_map.shape[0]
    devices = lax.axis_size("tok")
    ring, chips = ring_pairs(devices)
    swap = [(i, i ^ 1) for i in range(devices)]
    me = lax.axis_index("tok")
    labels = jnp.arange(experts, dtype=jnp.int32)
    my_expert = jnp.sum(jnp.where(owner_map == me, labels, 0), keepdims=True)
    block = packed(tokens, norm_gain, expert_ids, gate_weights, experts)

    total = None
    for step in range(chips):
        other = lax.ppermute(block, "tok", swap)
        here = block
        if step < chips - 1:
            block = lax.ppermute(block, "tok", ring)
        part, lent = visit(my_expert, here, other, experts, in_q, in_scale, down_q, down_scale)
        lent = lax.ppermute(lent, "tok", swap)
        part = part + lent.astype(jnp.float32)
        if step == 0:
            own = part
            continue
        if total is not None:
            part = part + total.astype(jnp.float32)
        total = lax.ppermute(part.astype(jnp.bfloat16), "tok", ring)
    return (own + total.astype(jnp.float32)).astype(jnp.bfloat16)


def solution(mesh):
    def on_device(tokens, norm_gain, expert_ids, gate_weights, owner_map, *blocks):
        tok_rows, experts = tokens.shape[0], owner_map.shape[0]
        mean_load = tok_rows * expert_ids.shape[1] // experts
        routed = experts * (mean_load + mean_load // 2)
        dense = tok_rows * mesh.shape["tok"]
        form = circulated if dense <= 2 * routed and mesh.shape["tok"] % 4 == 0 else exchanged
        return form(tokens, norm_gain, expert_ids, gate_weights, owner_map, *blocks)

    in_specs = (
        P(("grp", "tok"), None),
        P(),
        P(("grp", "tok"), None),
        P(("grp", "tok"), None),
        P(),
        P("tok", None, None, None),
        P("tok", None, None),
        P("tok", None, None),
        P("tok", None),
    )
    out_specs = P(("grp", "tok"), None)
    return jax.shard_map(
        on_device, mesh=mesh, in_specs=in_specs, out_specs=out_specs, check_vma=False
    )
```

```python
import functools

import jax
import jax.numpy as jnp
from jax import lax
from jax.experimental import pallas as pl
from jax.experimental.pallas import tpu as pltpu
from jax.sharding import PartitionSpec as P


TILE = 256
SMALL = 8 << 20
LARGE = 20 << 20


def expert_rows(batch_rows, in_blocks, in_scales, down_block, down_scales):
    gate_part = jnp.dot(batch_rows, in_blocks[0], preferred_element_type=jnp.float32) * in_scales[0]
    up_part = jnp.dot(batch_rows, in_blocks[1], preferred_element_type=jnp.float32) * in_scales[1]
    hidden = (jax.nn.silu(gate_part) * up_part).astype(jnp.bfloat16)
    return jnp.dot(hidden, down_block, preferred_element_type=jnp.float32) * down_scales


def normalized(tokens, norm_gain):
    values = tokens.astype(jnp.float32)
    row_scale = lax.rsqrt(jnp.mean(values * values, axis=1, keepdims=True) + 1e-06)
    return (values * row_scale * norm_gain).astype(jnp.bfloat16)


def exchanged(
    tokens, norm_gain, expert_ids, gate_weights, owner_map, in_q, in_scale, down_q, down_scale
):
    tok_rows, model_width = tokens.shape
    top_count = expert_ids.shape[1]
    experts = owner_map.shape[0]
    mean_load = tok_rows * top_count // experts
    capacity = mean_load + mean_load // 2
    normed = normalized(tokens, norm_gain)
    weights = gate_weights / jnp.sum(gate_weights, axis=1, keepdims=True)
    labels = jnp.arange(experts, dtype=jnp.int32)
    slot_table = jnp.sum(jnp.where(expert_ids[:, :, None] == labels, owner_map, 0), axis=2)
    flat_slot = slot_table.reshape(-1)
    onehot = (flat_slot[:, None] == labels).astype(jnp.int32)
    slot_rank = jnp.sum((jnp.cumsum(onehot, axis=0) - onehot) * onehot, axis=1)
    repeated = jnp.repeat(normed, top_count, axis=0)
    outgoing = (
        jnp.zeros((experts, capacity, model_width), jnp.bfloat16)
        .at[flat_slot, slot_rank]
        .set(repeated)
    )
    received = lax.all_to_all(outgoing, "tok", split_axis=0, concat_axis=0, tiled=True)
    source_count, slot_count, _ = received.shape
    flat_rows = received.reshape(source_count * slot_count, model_width)
    served = expert_rows(flat_rows, in_q[0], in_scale[0], down_q[0], down_scale[0])
    served = served.astype(jnp.bfloat16).reshape(source_count, slot_count, model_width)
    returned_rows = lax.all_to_all(served, "tok", split_axis=0, concat_axis=0, tiled=True)
    picked = returned_rows[flat_slot, slot_rank].reshape(tok_rows, top_count, model_width)
    mixed = jnp.sum(weights[:, :, None] * picked.astype(jnp.float32), axis=1)
    return mixed.astype(jnp.bfloat16)


def ring_pairs(devices):
    chips = devices // 2
    loop = list(range(0, chips, 2)) + list(range(chips - 1, 0, -2))
    pairs = []
    for place, chip in enumerate(loop):
        after = loop[(place + 1) % chips]
        pairs.append((2 * chip, 2 * after))
        pairs.append((2 * after + 1, 2 * chip + 1))
    return pairs, chips


def in_hbm(array):
    return pltpu.with_memory_space_constraint(array, pltpu.HBM)


def packed_kernel(experts, tokens_hbm, gain_hbm, ids_hbm, gates_hbm, out_ref, tokens, gain, ids, gates, sems):
    moves = [
        pltpu.make_async_copy(source, target, sems.at[i])
        for i, (source, target) in enumerate(
            ((ids_hbm, ids), (gates_hbm, gates), (tokens_hbm, tokens), (gain_hbm, gain))
        )
    ]
    for move in moves:
        move.start()
    tok_rows, model_width = tokens.shape
    lanes = out_ref.shape[1] - model_width
    moves[0].wait()
    moves[1].wait()
    weights = gates[...] / jnp.sum(gates[...], axis=0, keepdims=True)
    row = lax.broadcasted_iota(jnp.int32, (lanes, tok_rows), 0)
    label = jnp.where(row < experts, row, row - experts)
    table = jnp.zeros((lanes, tok_rows), jnp.float32)
    for k in range(ids.shape[0]):
        table += jnp.where(label == ids[k : k + 1, :], weights[k : k + 1, :], 0.0)
    high = table.astype(jnp.bfloat16).astype(jnp.float32)
    halves = jnp.where(row < experts, high, table - high)
    out_ref[:, model_width:] = jnp.transpose(halves).astype(jnp.bfloat16)
    moves[2].wait()
    moves[3].wait()
    values = tokens[...].astype(jnp.float32)
    row_scale = lax.rsqrt(jnp.mean(values * values, axis=1, keepdims=True) + 1e-06)
    out_ref[:, :model_width] = (values * row_scale * gain[...]).astype(jnp.bfloat16)


def packed(tokens, norm_gain, expert_ids, gate_weights, experts):
    tok_rows, model_width = tokens.shape
    top_count = expert_ids.shape[1]
    lanes = -(-2 * experts // 128) * 128
    return pl.pallas_call(
        functools.partial(packed_kernel, experts),
        out_shape=jax.ShapeDtypeStruct((tok_rows, model_width + lanes), jnp.bfloat16),
        in_specs=[pl.BlockSpec(memory_space=pltpu.HBM)] * 4,
        out_specs=pl.BlockSpec(memory_space=pltpu.VMEM),
        scratch_shapes=[
            pltpu.VMEM((tok_rows, model_width), jnp.bfloat16),
            pltpu.VMEM((1, model_width), jnp.float32),
            pltpu.VMEM((top_count, tok_rows), jnp.int32),
            pltpu.VMEM((top_count, tok_rows), jnp.float32),
            pltpu.SemaphoreType.DMA((4,)),
        ],
        compiler_params=pltpu.CompilerParams(vmem_limit_bytes=SMALL),
        name="packed",
    )(*map(in_hbm, (tokens, norm_gain[None, :], expert_ids.T, gate_weights.T)))


def loaded_kernel(
    owner_ref, in_hbm, in_scale_hbm, down_hbm, down_scale_hbm,
    mine_ref, in_ref, in_scale_ref, down_ref, down_scale_ref, sems,
):
    pairs = (
        (in_hbm, in_ref), (in_scale_hbm, in_scale_ref), (down_hbm, down_ref), (down_scale_hbm, down_scale_ref),
    )
    moves = [
        pltpu.make_async_copy(source, target, sems.at[i]) for i, (source, target) in enumerate(pairs)
    ]
    for move in moves:
        move.start()
    me = lax.axis_index("tok")
    mine_ref[0] = lax.fori_loop(
        0, owner_ref.shape[0], lambda i, found: jnp.where(owner_ref[i] == me, i, found), 0
    )
    for move in moves:
        move.wait()


def loaded(owner_map, in_q, in_scale, down_q, down_scale):
    blocks = (in_q, in_scale, down_q, down_scale)
    return pl.pallas_call(
        loaded_kernel,
        out_shape=(jax.ShapeDtypeStruct((1,), jnp.int32),)
        + tuple(jax.ShapeDtypeStruct(x.shape, x.dtype) for x in blocks),
        in_specs=[pl.BlockSpec(memory_space=pltpu.SMEM)] + [pl.BlockSpec(memory_space=pltpu.HBM)] * 4,
        out_specs=(pl.BlockSpec(memory_space=pltpu.SMEM),) + (pl.BlockSpec(memory_space=pltpu.VMEM),) * 4,
        scratch_shapes=[pltpu.SemaphoreType.DMA((4,))],
        compiler_params=pltpu.CompilerParams(vmem_limit_bytes=SMALL),
        cost_estimate=pl.CostEstimate(
            flops=0, bytes_accessed=2 * (in_q.size + down_q.size), transcendentals=0
        ),
        name="loaded",
    )(owner_map, *map(in_hbm, blocks))


def visit_kernel(
    experts, mine_ref, near_ref, far_ref, in_ref, in_scale_ref, down_ref, down_scale_ref,
    part_ref, lent_ref, rows_ref, hidden_ref,
):
    tok_rows, model_width = part_ref.shape
    hidden_width = hidden_ref.shape[1]
    rows_ref[:tok_rows] = near_ref[:, :model_width]
    rows_ref[tok_rows:] = far_ref[:, :model_width]
    rows = rows_ref[...]
    for start in range(0, hidden_width, TILE):
        cols = slice(start, start + TILE)
        gate = jnp.dot(rows, in_ref[0, 0, :, cols], preferred_element_type=jnp.float32)
        up = jnp.dot(rows, in_ref[0, 1, :, cols], preferred_element_type=jnp.float32)
        gate = gate * in_scale_ref[0, 0:1, cols].astype(jnp.float32)
        up = up * in_scale_ref[0, 1:2, cols].astype(jnp.float32)
        hidden_ref[:, cols] = (gate / (1.0 + jnp.exp(-gate)) * up).astype(jnp.bfloat16)
    lane = lax.broadcasted_iota(jnp.int32, (tok_rows, far_ref.shape[1] - model_width), 1)
    chosen = (lane == mine_ref[0]) | (lane == mine_ref[0] + experts)
    near = near_ref[:, model_width:].astype(jnp.float32)
    far = far_ref[:, model_width:].astype(jnp.float32)
    near_share = jnp.sum(jnp.where(chosen, near, 0.0), axis=1, keepdims=True)
    far_share = jnp.sum(jnp.where(chosen, far, 0.0), axis=1, keepdims=True)
    hidden = hidden_ref[...]
    for start in range(0, model_width, TILE):
        cols = slice(start, start + TILE)
        out = jnp.dot(hidden, down_ref[0, :, cols], preferred_element_type=jnp.float32)
        out = out * down_scale_ref[:, cols].astype(jnp.float32)
        part_ref[:, cols] = out[:tok_rows] * near_share
        lent_ref[:, cols] = (out[tok_rows:] * far_share).astype(jnp.bfloat16)


def visit(my_expert, near, far, experts, in_q, in_scale, down_q, down_scale):
    tok_rows = near.shape[0]
    hidden_width, model_width = down_q.shape[1:]
    flops = 2 * 2 * tok_rows * 3 * hidden_width * model_width
    return pl.pallas_call(
        functools.partial(visit_kernel, experts),
        out_shape=(
            jax.ShapeDtypeStruct((tok_rows, model_width), jnp.float32),
            jax.ShapeDtypeStruct((tok_rows, model_width), jnp.bfloat16),
        ),
        in_specs=[pl.BlockSpec(memory_space=pltpu.SMEM)]
        + [pl.BlockSpec(memory_space=pltpu.VMEM)] * 6,
        out_specs=(pl.BlockSpec(memory_space=pltpu.VMEM),) * 2,
        scratch_shapes=[
            pltpu.VMEM((2 * tok_rows, model_width), jnp.bfloat16),
            pltpu.VMEM((2 * tok_rows, hidden_width), jnp.bfloat16),
        ],
        compiler_params=pltpu.CompilerParams(vmem_limit_bytes=LARGE),
        cost_estimate=pl.CostEstimate(
            flops=flops, bytes_accessed=6 * tok_rows * model_width, transcendentals=0
        ),
        name="visit",
    )(my_expert, near, far, in_q, in_scale, down_q, down_scale)


def circulated(
    tokens, norm_gain, expert_ids, gate_weights, owner_map, in_q, in_scale, down_q, down_scale
):
    experts = owner_map.shape[0]
    devices = lax.axis_size("tok")
    ring, chips = ring_pairs(devices)
    swap = [(i, i ^ 1) for i in range(devices)]
    half = tokens.shape[0] // 2
    block = packed(tokens, norm_gain, expert_ids, gate_weights, experts)
    mine, *blocks = loaded(owner_map, in_q, in_scale, down_q, down_scale)

    parts = []
    for step in range(chips):
        other = lax.ppermute(block, "tok", swap)
        here = block
        if step < chips - 1:
            block = lax.ppermute(block, "tok", ring)
        part, lent = visit(mine, here, other, experts, *blocks)
        parts.append((part, lax.ppermute(lent, "tok", swap)))

    total = None
    for step in range(1, chips):
        part, lent = parts[step]
        cuts = (slice(None),) if step < chips - 2 else (slice(0, half), slice(half, None))
        if total is not None and len(total) < len(cuts):
            total = [total[0][cut] for cut in cuts]
        sums = [part[cut] + lent[cut].astype(jnp.float32) for cut in cuts]
        if total is not None:
            sums = [x + y.astype(jnp.float32) for x, y in zip(sums, total)]
        total = [lax.ppermute(x.astype(jnp.bfloat16), "tok", ring) for x in sums]
    part, lent = parts[0]
    return jnp.concatenate(
        [
            (part[cut] + lent[cut].astype(jnp.float32) + x.astype(jnp.float32)).astype(jnp.bfloat16)
            for cut, x in zip((slice(0, half), slice(half, None)), total)
        ]
    )


def solution(mesh):
    devices = mesh.shape["tok"]
    row = P(("grp", "tok"), None)
    slot = [P("tok", *(None,) * extra) for extra in (3, 2, 2, 1)]

    def placed(body):
        return jax.shard_map(
            body,
            mesh=mesh,
            in_specs=(row, P(), row, row, P(), *slot),
            out_specs=row,
            check_vma=False,
        )


    def step(tokens, norm_gain, expert_ids, gate_weights, owner_map, *blocks):
        tok_rows = tokens.shape[0] // mesh.size
        experts = owner_map.shape[0]
        mean_load = tok_rows * expert_ids.shape[1] // experts
        routed = experts * (mean_load + mean_load // 2)
        arguments = (tokens, norm_gain, expert_ids, gate_weights, owner_map, *blocks)
        if tok_rows * devices > 2 * routed or devices % 4:
            return placed(exchanged)(*arguments)
        return placed(circulated)(*arguments)

    return step
```

```python
import functools

import jax
import jax.numpy as jnp
from jax import lax
from jax.experimental import pallas as pl
from jax.experimental.pallas import tpu as pltpu
from jax.sharding import PartitionSpec as P


TILE = 256
SMALL = 8 << 20
LARGE = 20 << 20


def expert_rows(batch_rows, in_blocks, in_scales, down_block, down_scales):
    gate_part = jnp.dot(batch_rows, in_blocks[0], preferred_element_type=jnp.float32) * in_scales[0]
    up_part = jnp.dot(batch_rows, in_blocks[1], preferred_element_type=jnp.float32) * in_scales[1]
    hidden = (jax.nn.silu(gate_part) * up_part).astype(jnp.bfloat16)
    return jnp.dot(hidden, down_block, preferred_element_type=jnp.float32) * down_scales


def normalized(tokens, norm_gain):
    values = tokens.astype(jnp.float32)
    row_scale = lax.rsqrt(jnp.mean(values * values, axis=1, keepdims=True) + 1e-06)
    return (values * row_scale * norm_gain).astype(jnp.bfloat16)


def exchanged(
    tokens, norm_gain, expert_ids, gate_weights, owner_map, in_q, in_scale, down_q, down_scale
):
    tok_rows, model_width = tokens.shape
    top_count = expert_ids.shape[1]
    experts = owner_map.shape[0]
    mean_load = tok_rows * top_count // experts
    capacity = mean_load + mean_load // 2
    normed = normalized(tokens, norm_gain)
    weights = gate_weights / jnp.sum(gate_weights, axis=1, keepdims=True)
    labels = jnp.arange(experts, dtype=jnp.int32)
    slot_table = jnp.sum(jnp.where(expert_ids[:, :, None] == labels, owner_map, 0), axis=2)
    flat_slot = slot_table.reshape(-1)
    onehot = (flat_slot[:, None] == labels).astype(jnp.int32)
    slot_rank = jnp.sum((jnp.cumsum(onehot, axis=0) - onehot) * onehot, axis=1)
    repeated = jnp.repeat(normed, top_count, axis=0)
    outgoing = (
        jnp.zeros((experts, capacity, model_width), jnp.bfloat16)
        .at[flat_slot, slot_rank]
        .set(repeated)
    )
    received = lax.all_to_all(outgoing, "tok", split_axis=0, concat_axis=0, tiled=True)
    source_count, slot_count, _ = received.shape
    flat_rows = received.reshape(source_count * slot_count, model_width)
    served = expert_rows(flat_rows, in_q[0], in_scale[0], down_q[0], down_scale[0])
    served = served.astype(jnp.bfloat16).reshape(source_count, slot_count, model_width)
    returned_rows = lax.all_to_all(served, "tok", split_axis=0, concat_axis=0, tiled=True)
    picked = returned_rows[flat_slot, slot_rank].reshape(tok_rows, top_count, model_width)
    mixed = jnp.sum(weights[:, :, None] * picked.astype(jnp.float32), axis=1)
    return mixed.astype(jnp.bfloat16)


def ring_pairs(devices):
    chips = devices // 2
    loop = list(range(0, chips, 2)) + list(range(chips - 1, 0, -2))
    pairs = []
    for place, chip in enumerate(loop):
        after = loop[(place + 1) % chips]
        pairs.append((2 * chip, 2 * after))
        pairs.append((2 * after + 1, 2 * chip + 1))
    return pairs, chips


def in_hbm(array):
    return pltpu.with_memory_space_constraint(array, pltpu.HBM)


def packed_kernel(experts, tokens_hbm, gain_hbm, ids_hbm, gates_hbm, out_ref, tokens, gain, ids, gates, sems):
    moves = [
        pltpu.make_async_copy(source, target, sems.at[i])
        for i, (source, target) in enumerate(
            ((ids_hbm, ids), (gates_hbm, gates), (tokens_hbm, tokens), (gain_hbm, gain))
        )
    ]
    for move in moves:
        move.start()
    tok_rows, model_width = tokens.shape
    lanes = out_ref.shape[1] - model_width
    moves[0].wait()
    moves[1].wait()
    weights = gates[...] / jnp.sum(gates[...], axis=0, keepdims=True)
    row = lax.broadcasted_iota(jnp.int32, (lanes, tok_rows), 0)
    label = jnp.where(row < experts, row, row - experts)
    table = jnp.zeros((lanes, tok_rows), jnp.float32)
    for k in range(ids.shape[0]):
        table += jnp.where(label == ids[k : k + 1, :], weights[k : k + 1, :], 0.0)
    high = table.astype(jnp.bfloat16).astype(jnp.float32)
    halves = jnp.where(row < experts, high, table - high)
    out_ref[:, model_width:] = jnp.transpose(halves).astype(jnp.bfloat16)
    moves[2].wait()
    moves[3].wait()
    values = tokens[...].astype(jnp.float32)
    row_scale = lax.rsqrt(jnp.mean(values * values, axis=1, keepdims=True) + 1e-06)
    out_ref[:, :model_width] = (values * row_scale * gain[...]).astype(jnp.bfloat16)


def packed(tokens, norm_gain, expert_ids, gate_weights, experts):
    tok_rows, model_width = tokens.shape
    top_count = expert_ids.shape[1]
    lanes = -(-2 * experts // 128) * 128
    return pl.pallas_call(
        functools.partial(packed_kernel, experts),
        out_shape=jax.ShapeDtypeStruct((tok_rows, model_width + lanes), jnp.bfloat16),
        in_specs=[pl.BlockSpec(memory_space=pltpu.HBM)] * 4,
        out_specs=pl.BlockSpec(memory_space=pltpu.VMEM),
        scratch_shapes=[
            pltpu.VMEM((tok_rows, model_width), jnp.bfloat16),
            pltpu.VMEM((1, model_width), jnp.float32),
            pltpu.VMEM((top_count, tok_rows), jnp.int32),
            pltpu.VMEM((top_count, tok_rows), jnp.float32),
            pltpu.SemaphoreType.DMA((4,)),
        ],
        compiler_params=pltpu.CompilerParams(vmem_limit_bytes=SMALL),
        name="packed",
    )(*map(in_hbm, (tokens, norm_gain[None, :], expert_ids.T, gate_weights.T)))


def loaded_kernel(
    owner_ref, in_hbm, in_scale_hbm, down_hbm, down_scale_hbm,
    mine_ref, in_ref, in_scale_ref, down_ref, down_scale_ref, sems,
):
    pairs = (
        (in_hbm, in_ref), (in_scale_hbm, in_scale_ref), (down_hbm, down_ref), (down_scale_hbm, down_scale_ref),
    )
    moves = [
        pltpu.make_async_copy(source, target, sems.at[i]) for i, (source, target) in enumerate(pairs)
    ]
    for move in moves:
        move.start()
    me = lax.axis_index("tok")
    mine_ref[0] = lax.fori_loop(
        0, owner_ref.shape[0], lambda i, found: jnp.where(owner_ref[i] == me, i, found), 0
    )
    for move in moves:
        move.wait()


def loaded(owner_map, in_q, in_scale, down_q, down_scale):
    blocks = (in_q, in_scale, down_q, down_scale)
    return pl.pallas_call(
        loaded_kernel,
        out_shape=(jax.ShapeDtypeStruct((1,), jnp.int32),)
        + tuple(jax.ShapeDtypeStruct(x.shape, x.dtype) for x in blocks),
        in_specs=[pl.BlockSpec(memory_space=pltpu.SMEM)] + [pl.BlockSpec(memory_space=pltpu.HBM)] * 4,
        out_specs=(pl.BlockSpec(memory_space=pltpu.SMEM),) + (pl.BlockSpec(memory_space=pltpu.VMEM),) * 4,
        scratch_shapes=[pltpu.SemaphoreType.DMA((4,))],
        compiler_params=pltpu.CompilerParams(vmem_limit_bytes=SMALL),
        cost_estimate=pl.CostEstimate(
            flops=0, bytes_accessed=2 * (in_q.size + down_q.size), transcendentals=0
        ),
        name="loaded",
    )(owner_map, *map(in_hbm, blocks))


def visit_kernel(
    experts, mine_ref, near_ref, far_ref, in_ref, in_scale_ref, down_ref, down_scale_ref,
    part_ref, lent_ref, rows_ref, hidden_ref,
):
    tok_rows, model_width = part_ref.shape
    hidden_width = hidden_ref.shape[1]
    rows_ref[:tok_rows] = near_ref[:, :model_width]
    rows_ref[tok_rows:] = far_ref[:, :model_width]
    rows = rows_ref[...]
    for start in range(0, hidden_width, TILE):
        cols = slice(start, start + TILE)
        gate = jnp.dot(rows, in_ref[0, 0, :, cols], preferred_element_type=jnp.float32)
        up = jnp.dot(rows, in_ref[0, 1, :, cols], preferred_element_type=jnp.float32)
        gate = gate * in_scale_ref[0, 0:1, cols].astype(jnp.float32)
        up = up * in_scale_ref[0, 1:2, cols].astype(jnp.float32)
        hidden_ref[:, cols] = (gate / (1.0 + jnp.exp(-gate)) * up).astype(jnp.bfloat16)
    lane = lax.broadcasted_iota(jnp.int32, (tok_rows, far_ref.shape[1] - model_width), 1)
    chosen = (lane == mine_ref[0]) | (lane == mine_ref[0] + experts)
    near = near_ref[:, model_width:].astype(jnp.float32)
    far = far_ref[:, model_width:].astype(jnp.float32)
    near_share = jnp.sum(jnp.where(chosen, near, 0.0), axis=1, keepdims=True)
    far_share = jnp.sum(jnp.where(chosen, far, 0.0), axis=1, keepdims=True)
    hidden = hidden_ref[...]
    for start in range(0, model_width, TILE):
        cols = slice(start, start + TILE)
        out = jnp.dot(hidden, down_ref[0, :, cols], preferred_element_type=jnp.float32)
        out = out * down_scale_ref[:, cols].astype(jnp.float32)
        part_ref[:, cols] = out[:tok_rows] * near_share
        lent_ref[:, cols] = (out[tok_rows:] * far_share).astype(jnp.bfloat16)


def visit(my_expert, near, far, experts, in_q, in_scale, down_q, down_scale):
    tok_rows = near.shape[0]
    hidden_width, model_width = down_q.shape[1:]
    flops = 2 * 2 * tok_rows * 3 * hidden_width * model_width
    return pl.pallas_call(
        functools.partial(visit_kernel, experts),
        out_shape=(
            jax.ShapeDtypeStruct((tok_rows, model_width), jnp.float32),
            jax.ShapeDtypeStruct((tok_rows, model_width), jnp.bfloat16),
        ),
        in_specs=[pl.BlockSpec(memory_space=pltpu.SMEM)]
        + [pl.BlockSpec(memory_space=pltpu.VMEM)] * 6,
        out_specs=(pl.BlockSpec(memory_space=pltpu.VMEM),) * 2,
        scratch_shapes=[
            pltpu.VMEM((2 * tok_rows, model_width), jnp.bfloat16),
            pltpu.VMEM((2 * tok_rows, hidden_width), jnp.bfloat16),
        ],
        compiler_params=pltpu.CompilerParams(vmem_limit_bytes=LARGE),
        cost_estimate=pl.CostEstimate(
            flops=flops, bytes_accessed=6 * tok_rows * model_width, transcendentals=0
        ),
        name="visit",
    )(my_expert, near, far, in_q, in_scale, down_q, down_scale)


def circulated(
    tokens, norm_gain, expert_ids, gate_weights, owner_map, in_q, in_scale, down_q, down_scale
):
    experts = owner_map.shape[0]
    devices = lax.axis_size("tok")
    ring, chips = ring_pairs(devices)
    swap = [(i, i ^ 1) for i in range(devices)]
    half = tokens.shape[0] // 2
    block = packed(tokens, norm_gain, expert_ids, gate_weights, experts)
    mine, *blocks = loaded(owner_map, in_q, in_scale, down_q, down_scale)

    parts = []
    for step in range(chips):
        here = block
        other = lax.ppermute(here, "tok", swap)
        if step < chips - 1:
            block = lax.ppermute(here, "tok", ring)
        part, lent = visit(mine, here, other, experts, *blocks)
        parts.append((part, lax.ppermute(lent, "tok", swap)))

    def summed(step, cut, arrived):
        part, lent = (x[cut].astype(jnp.float32) for x in parts[step])
        return (part + lent + arrived.astype(jnp.float32)).astype(jnp.bfloat16)

    total = jnp.zeros((), jnp.bfloat16)
    for step in range(1, chips - 2):
        total = lax.ppermute(summed(step, slice(None), total), "tok", ring)
    halves = {"a": slice(0, half), "b": slice(half, None)}
    totals = {name: total[cut] for name, cut in halves.items()}
    for step in range(chips - 2, chips):
        for name, cut in halves.items():
            totals[name] = lax.ppermute(summed(step, cut, totals[name]), "tok", ring)
    return jnp.concatenate([summed(0, cut, totals[name]) for name, cut in halves.items()])


def solution(mesh):
    devices = mesh.shape["tok"]
    row = P(("grp", "tok"), None)
    slot = [P("tok", *(None,) * extra) for extra in (3, 2, 2, 1)]

    def placed(body):
        return jax.shard_map(
            body,
            mesh=mesh,
            in_specs=(row, P(), row, row, P(), *slot),
            out_specs=row,
            check_vma=False,
        )

    def step(tokens, norm_gain, expert_ids, gate_weights, owner_map, *blocks):
        tok_rows = tokens.shape[0] // mesh.size
        experts = owner_map.shape[0]
        mean_load = tok_rows * expert_ids.shape[1] // experts
        routed = experts * (mean_load + mean_load // 2)
        arguments = (tokens, norm_gain, expert_ids, gate_weights, owner_map, *blocks)
        if tok_rows * devices > 2 * routed or devices % 4:
            return placed(exchanged)(*arguments)
        return placed(circulated)(*arguments)

    return step
```

```python
import functools

import jax
import jax.numpy as jnp
from jax import lax
from jax.experimental import pallas as pl
from jax.experimental.pallas import tpu as pltpu
from jax.sharding import PartitionSpec as P


TILE = 256
SMALL = 8 << 20
LARGE = 20 << 20


def expert_rows(batch_rows, in_blocks, in_scales, down_block, down_scales):
    gate_part = jnp.dot(batch_rows, in_blocks[0], preferred_element_type=jnp.float32) * in_scales[0]
    up_part = jnp.dot(batch_rows, in_blocks[1], preferred_element_type=jnp.float32) * in_scales[1]
    hidden = (jax.nn.silu(gate_part) * up_part).astype(jnp.bfloat16)
    return jnp.dot(hidden, down_block, preferred_element_type=jnp.float32) * down_scales


def normalized(tokens, norm_gain):
    values = tokens.astype(jnp.float32)
    row_scale = lax.rsqrt(jnp.mean(values * values, axis=1, keepdims=True) + 1e-06)
    return (values * row_scale * norm_gain).astype(jnp.bfloat16)


def exchanged(
    tokens, norm_gain, expert_ids, gate_weights, owner_map, in_q, in_scale, down_q, down_scale
):
    tok_rows, model_width = tokens.shape
    top_count = expert_ids.shape[1]
    experts = owner_map.shape[0]
    mean_load = tok_rows * top_count // experts
    capacity = mean_load + mean_load // 2
    normed = normalized(tokens, norm_gain)
    weights = gate_weights / jnp.sum(gate_weights, axis=1, keepdims=True)
    labels = jnp.arange(experts, dtype=jnp.int32)
    slot_table = jnp.sum(jnp.where(expert_ids[:, :, None] == labels, owner_map, 0), axis=2)
    flat_slot = slot_table.reshape(-1)
    onehot = (flat_slot[:, None] == labels).astype(jnp.int32)
    slot_rank = jnp.sum((jnp.cumsum(onehot, axis=0) - onehot) * onehot, axis=1)
    repeated = jnp.repeat(normed, top_count, axis=0)
    outgoing = (
        jnp.zeros((experts, capacity, model_width), jnp.bfloat16)
        .at[flat_slot, slot_rank]
        .set(repeated)
    )
    received = lax.all_to_all(outgoing, "tok", split_axis=0, concat_axis=0, tiled=True)
    source_count, slot_count, _ = received.shape
    flat_rows = received.reshape(source_count * slot_count, model_width)
    served = expert_rows(flat_rows, in_q[0], in_scale[0], down_q[0], down_scale[0])
    served = served.astype(jnp.bfloat16).reshape(source_count, slot_count, model_width)
    returned_rows = lax.all_to_all(served, "tok", split_axis=0, concat_axis=0, tiled=True)
    picked = returned_rows[flat_slot, slot_rank].reshape(tok_rows, top_count, model_width)
    mixed = jnp.sum(weights[:, :, None] * picked.astype(jnp.float32), axis=1)
    return mixed.astype(jnp.bfloat16)


def ring_pairs(devices):
    chips = devices // 2
    loop = list(range(0, chips, 2)) + list(range(chips - 1, 0, -2))
    pairs = []
    for place, chip in enumerate(loop):
        after = loop[(place + 1) % chips]
        pairs.append((2 * chip, 2 * after))
        pairs.append((2 * after + 1, 2 * chip + 1))
    return pairs, chips


def in_hbm(array):
    return pltpu.with_memory_space_constraint(array, pltpu.HBM)


def packed_kernel(experts, tokens_hbm, gain_hbm, ids_hbm, gates_hbm, out_ref, tokens, gain, ids, gates, sems):
    moves = [
        pltpu.make_async_copy(source, target, sems.at[i])
        for i, (source, target) in enumerate(
            ((ids_hbm, ids), (gates_hbm, gates), (tokens_hbm, tokens), (gain_hbm, gain))
        )
    ]
    for move in moves:
        move.start()
    tok_rows, model_width = tokens.shape
    lanes = out_ref.shape[1] - model_width
    moves[0].wait()
    moves[1].wait()
    weights = gates[...] / jnp.sum(gates[...], axis=0, keepdims=True)
    row = lax.broadcasted_iota(jnp.int32, (lanes, tok_rows), 0)
    label = jnp.where(row < experts, row, row - experts)
    table = jnp.zeros((lanes, tok_rows), jnp.float32)
    for k in range(ids.shape[0]):
        table += jnp.where(label == ids[k : k + 1, :], weights[k : k + 1, :], 0.0)
    high = table.astype(jnp.bfloat16).astype(jnp.float32)
    halves = jnp.where(row < experts, high, table - high)
    out_ref[:, model_width:] = jnp.transpose(halves).astype(jnp.bfloat16)
    moves[2].wait()
    moves[3].wait()
    values = tokens[...].astype(jnp.float32)
    row_scale = lax.rsqrt(jnp.mean(values * values, axis=1, keepdims=True) + 1e-06)
    out_ref[:, :model_width] = (values * row_scale * gain[...]).astype(jnp.bfloat16)


def packed(tokens, norm_gain, expert_ids, gate_weights, experts):
    tok_rows, model_width = tokens.shape
    top_count = expert_ids.shape[1]
    lanes = -(-2 * experts // 128) * 128
    return pl.pallas_call(
        functools.partial(packed_kernel, experts),
        out_shape=jax.ShapeDtypeStruct((tok_rows, model_width + lanes), jnp.bfloat16),
        in_specs=[pl.BlockSpec(memory_space=pltpu.HBM)] * 4,
        out_specs=pl.BlockSpec(memory_space=pltpu.VMEM),
        scratch_shapes=[
            pltpu.VMEM((tok_rows, model_width), jnp.bfloat16),
            pltpu.VMEM((1, model_width), jnp.float32),
            pltpu.VMEM((top_count, tok_rows), jnp.int32),
            pltpu.VMEM((top_count, tok_rows), jnp.float32),
            pltpu.SemaphoreType.DMA((4,)),
        ],
        compiler_params=pltpu.CompilerParams(vmem_limit_bytes=SMALL),
        name="packed",
    )(*map(in_hbm, (tokens, norm_gain[None, :], expert_ids.T, gate_weights.T)))


def found_kernel(owner_ref, mine_ref):
    me = lax.axis_index("tok")
    mine_ref[0] = lax.fori_loop(
        0, owner_ref.shape[0], lambda i, found: jnp.where(owner_ref[i] == me, i, found), 0
    )


def loaded_kernel(count, *refs):
    sources, targets, sems = refs[:count], refs[count : 2 * count], refs[-1]
    moves = [
        pltpu.make_async_copy(source, target, sems.at[i])
        for i, (source, target) in enumerate(zip(sources, targets))
    ]
    for move in moves:
        move.start()
    for move in moves:
        move.wait()


def loaded(*arrays):
    count = len(arrays)
    return pl.pallas_call(
        functools.partial(loaded_kernel, count),
        out_shape=tuple(jax.ShapeDtypeStruct(x.shape, x.dtype) for x in arrays),
        in_specs=[pl.BlockSpec(memory_space=pltpu.HBM)] * count,
        out_specs=(pl.BlockSpec(memory_space=pltpu.VMEM),) * count,
        scratch_shapes=[pltpu.SemaphoreType.DMA((count,))],
        compiler_params=pltpu.CompilerParams(vmem_limit_bytes=SMALL),
        cost_estimate=pl.CostEstimate(
            flops=0, bytes_accessed=2 * sum(x.size for x in arrays), transcendentals=0
        ),
        name="loaded",
    )(*map(in_hbm, arrays))


def visit_kernel(
    experts, mine_ref, near_ref, far_ref, in_ref, in_scale_ref, down_ref, down_scale_ref,
    part_ref, lent_ref, rows_ref, hidden_ref,
):
    tok_rows, model_width = part_ref.shape
    hidden_width = hidden_ref.shape[1]
    rows_ref[:tok_rows] = near_ref[:, :model_width]
    rows_ref[tok_rows:] = far_ref[:, :model_width]
    rows = rows_ref[...]
    for start in range(0, hidden_width, TILE):
        cols = slice(start, start + TILE)
        gate = jnp.dot(rows, in_ref[0, 0, :, cols], preferred_element_type=jnp.float32)
        up = jnp.dot(rows, in_ref[0, 1, :, cols], preferred_element_type=jnp.float32)
        gate = gate * in_scale_ref[0, 0:1, cols].astype(jnp.float32)
        up = up * in_scale_ref[0, 1:2, cols].astype(jnp.float32)
        hidden_ref[:, cols] = (gate / (1.0 + jnp.exp(-gate)) * up).astype(jnp.bfloat16)
    lane = lax.broadcasted_iota(jnp.int32, (tok_rows, far_ref.shape[1] - model_width), 1)
    chosen = (lane == mine_ref[0]) | (lane == mine_ref[0] + experts)
    near = near_ref[:, model_width:].astype(jnp.float32)
    far = far_ref[:, model_width:].astype(jnp.float32)
    near_share = jnp.sum(jnp.where(chosen, near, 0.0), axis=1, keepdims=True)
    far_share = jnp.sum(jnp.where(chosen, far, 0.0), axis=1, keepdims=True)
    hidden = hidden_ref[...]
    for start in range(0, model_width, TILE):
        cols = slice(start, start + TILE)
        out = jnp.dot(hidden, down_ref[0, :, cols], preferred_element_type=jnp.float32)
        out = out * down_scale_ref[:, cols].astype(jnp.float32)
        part_ref[:, cols] = out[:tok_rows] * near_share
        lent_ref[:, cols] = (out[tok_rows:] * far_share).astype(jnp.bfloat16)


def visit(my_expert, near, far, experts, in_q, in_scale, down_q, down_scale):
    tok_rows = near.shape[0]
    hidden_width, model_width = down_q.shape[1:]
    flops = 2 * 2 * tok_rows * 3 * hidden_width * model_width
    return pl.pallas_call(
        functools.partial(visit_kernel, experts),
        out_shape=(
            jax.ShapeDtypeStruct((tok_rows, model_width), jnp.float32),
            jax.ShapeDtypeStruct((tok_rows, model_width), jnp.bfloat16),
        ),
        in_specs=[pl.BlockSpec(memory_space=pltpu.SMEM)]
        + [pl.BlockSpec(memory_space=pltpu.VMEM)] * 6,
        out_specs=(pl.BlockSpec(memory_space=pltpu.VMEM),) * 2,
        scratch_shapes=[
            pltpu.VMEM((2 * tok_rows, model_width), jnp.bfloat16),
            pltpu.VMEM((2 * tok_rows, hidden_width), jnp.bfloat16),
        ],
        compiler_params=pltpu.CompilerParams(vmem_limit_bytes=LARGE),
        cost_estimate=pl.CostEstimate(
            flops=flops, bytes_accessed=6 * tok_rows * model_width, transcendentals=0
        ),
        name="visit",
    )(my_expert, near, far, in_q, in_scale, down_q, down_scale)


def circulated(
    tokens, norm_gain, expert_ids, gate_weights, owner_map, in_q, in_scale, down_q, down_scale
):
    experts = owner_map.shape[0]
    devices = lax.axis_size("tok")
    ring, chips = ring_pairs(devices)
    swap = [(i, i ^ 1) for i in range(devices)]
    half = tokens.shape[0] // 2
    block = packed(tokens, norm_gain, expert_ids, gate_weights, experts)
    blocks = loaded(in_q, in_scale, down_q, down_scale)
    mine = pl.pallas_call(
        found_kernel,
        out_shape=jax.ShapeDtypeStruct((1,), jnp.int32),
        in_specs=[pl.BlockSpec(memory_space=pltpu.SMEM)],
        out_specs=pl.BlockSpec(memory_space=pltpu.SMEM),
        compiler_params=pltpu.CompilerParams(vmem_limit_bytes=SMALL),
        name="found",
    )(owner_map)

    back = lax.ppermute(block, "tok", [(target, source) for source, target in ring])
    parts = []
    for step in range(chips):
        here = block if step < chips - 1 else back
        other = lax.ppermute(here, "tok", swap)
        if step < chips - 2:
            block = lax.ppermute(here, "tok", ring)
        part, lent = visit(mine, here, other, experts, *blocks)
        parts.append((part, lax.ppermute(lent, "tok", swap)))

    def summed(step, cut, arrived):
        part, lent = (x[cut].astype(jnp.float32) for x in parts[step])
        return (part + lent + arrived.astype(jnp.float32)).astype(jnp.bfloat16)

    total = jnp.zeros((), jnp.bfloat16)
    for step in range(1, chips - 2):
        total = lax.ppermute(summed(step, slice(None), total), "tok", ring)
    halves = {"a": slice(0, half), "b": slice(half, None)}
    totals = {name: total[cut] for name, cut in halves.items()}
    for step in range(chips - 2, chips):
        for name, cut in halves.items():
            totals[name] = lax.ppermute(summed(step, cut, totals[name]), "tok", ring)
    return jnp.concatenate([summed(0, cut, totals[name]) for name, cut in halves.items()])


def solution(mesh):
    devices = mesh.shape["tok"]
    row = P(("grp", "tok"), None)
    slot = [P("tok", *(None,) * extra) for extra in (3, 2, 2, 1)]

    def placed(body):
        return jax.shard_map(
            body,
            mesh=mesh,
            in_specs=(row, P(), row, row, P(), *slot),
            out_specs=row,
            check_vma=False,
        )

    def step(tokens, norm_gain, expert_ids, gate_weights, owner_map, *blocks):
        tok_rows = tokens.shape[0] // mesh.size
        experts = owner_map.shape[0]
        mean_load = tok_rows * expert_ids.shape[1] // experts
        routed = experts * (mean_load + mean_load // 2)
        arguments = (tokens, norm_gain, expert_ids, gate_weights, owner_map, *blocks)
        if tok_rows * devices > 2 * routed or devices % 4:
            return placed(exchanged)(*arguments)
        return placed(circulated)(*arguments)

    return step
```

```python
import functools

import jax
import jax.numpy as jnp
from jax import lax
from jax.experimental import pallas as pl
from jax.experimental.pallas import tpu as pltpu
from jax.sharding import PartitionSpec as P


TILE = 256
SMALL = 8 << 20
LARGE = 20 << 20


def expert_rows(batch_rows, in_blocks, in_scales, down_block, down_scales):
    gate_part = jnp.dot(batch_rows, in_blocks[0], preferred_element_type=jnp.float32) * in_scales[0]
    up_part = jnp.dot(batch_rows, in_blocks[1], preferred_element_type=jnp.float32) * in_scales[1]
    hidden = (jax.nn.silu(gate_part) * up_part).astype(jnp.bfloat16)
    return jnp.dot(hidden, down_block, preferred_element_type=jnp.float32) * down_scales


def normalized(tokens, norm_gain):
    values = tokens.astype(jnp.float32)
    row_scale = lax.rsqrt(jnp.mean(values * values, axis=1, keepdims=True) + 1e-06)
    return (values * row_scale * norm_gain).astype(jnp.bfloat16)


def exchanged(
    tokens, norm_gain, expert_ids, gate_weights, owner_map, in_q, in_scale, down_q, down_scale
):
    tok_rows, model_width = tokens.shape
    top_count = expert_ids.shape[1]
    experts = owner_map.shape[0]
    mean_load = tok_rows * top_count // experts
    capacity = mean_load + mean_load // 2
    normed = normalized(tokens, norm_gain)
    weights = gate_weights / jnp.sum(gate_weights, axis=1, keepdims=True)
    labels = jnp.arange(experts, dtype=jnp.int32)
    slot_table = jnp.sum(jnp.where(expert_ids[:, :, None] == labels, owner_map, 0), axis=2)
    flat_slot = slot_table.reshape(-1)
    onehot = (flat_slot[:, None] == labels).astype(jnp.int32)
    slot_rank = jnp.sum((jnp.cumsum(onehot, axis=0) - onehot) * onehot, axis=1)
    repeated = jnp.repeat(normed, top_count, axis=0)
    outgoing = (
        jnp.zeros((experts, capacity, model_width), jnp.bfloat16)
        .at[flat_slot, slot_rank]
        .set(repeated)
    )
    received = lax.all_to_all(outgoing, "tok", split_axis=0, concat_axis=0, tiled=True)
    source_count, slot_count, _ = received.shape
    flat_rows = received.reshape(source_count * slot_count, model_width)
    served = expert_rows(flat_rows, in_q[0], in_scale[0], down_q[0], down_scale[0])
    served = served.astype(jnp.bfloat16).reshape(source_count, slot_count, model_width)
    returned_rows = lax.all_to_all(served, "tok", split_axis=0, concat_axis=0, tiled=True)
    picked = returned_rows[flat_slot, slot_rank].reshape(tok_rows, top_count, model_width)
    mixed = jnp.sum(weights[:, :, None] * picked.astype(jnp.float32), axis=1)
    return mixed.astype(jnp.bfloat16)


def ring_pairs(devices):
    chips = devices // 2
    loop = list(range(0, chips, 2)) + list(range(chips - 1, 0, -2))
    pairs = []
    for place, chip in enumerate(loop):
        after = loop[(place + 1) % chips]
        pairs.append((2 * chip, 2 * after))
        pairs.append((2 * after + 1, 2 * chip + 1))
    return pairs, chips


def in_hbm(array):
    return pltpu.with_memory_space_constraint(array, pltpu.HBM)


def packed_kernel(experts, tokens_hbm, gain_hbm, ids_hbm, gates_hbm, out_ref, tokens, gain, ids, gates, sems):
    moves = [
        pltpu.make_async_copy(source, target, sems.at[i])
        for i, (source, target) in enumerate(
            ((ids_hbm, ids), (gates_hbm, gates), (tokens_hbm, tokens), (gain_hbm, gain))
        )
    ]
    for move in moves:
        move.start()
    tok_rows, model_width = tokens.shape
    lanes = out_ref.shape[1] - model_width
    moves[0].wait()
    moves[1].wait()
    weights = gates[...] / jnp.sum(gates[...], axis=0, keepdims=True)
    row = lax.broadcasted_iota(jnp.int32, (lanes, tok_rows), 0)
    label = jnp.where(row < experts, row, row - experts)
    table = jnp.zeros((lanes, tok_rows), jnp.float32)
    for k in range(ids.shape[0]):
        table += jnp.where(label == ids[k : k + 1, :], weights[k : k + 1, :], 0.0)
    high = table.astype(jnp.bfloat16).astype(jnp.float32)
    halves = jnp.where(row < experts, high, table - high)
    out_ref[:, model_width:] = jnp.transpose(halves).astype(jnp.bfloat16)
    moves[2].wait()
    moves[3].wait()
    values = tokens[...].astype(jnp.float32)
    row_scale = lax.rsqrt(jnp.mean(values * values, axis=1, keepdims=True) + 1e-06)
    out_ref[:, :model_width] = (values * row_scale * gain[...]).astype(jnp.bfloat16)


def packed(tokens, norm_gain, expert_ids, gate_weights, experts):
    tok_rows, model_width = tokens.shape
    top_count = expert_ids.shape[1]
    lanes = -(-2 * experts // 128) * 128
    return pl.pallas_call(
        functools.partial(packed_kernel, experts),
        out_shape=jax.ShapeDtypeStruct((tok_rows, model_width + lanes), jnp.bfloat16),
        in_specs=[pl.BlockSpec(memory_space=pltpu.HBM)] * 4,
        out_specs=pl.BlockSpec(memory_space=pltpu.VMEM),
        scratch_shapes=[
            pltpu.VMEM((tok_rows, model_width), jnp.bfloat16),
            pltpu.VMEM((1, model_width), jnp.float32),
            pltpu.VMEM((top_count, tok_rows), jnp.int32),
            pltpu.VMEM((top_count, tok_rows), jnp.float32),
            pltpu.SemaphoreType.DMA((4,)),
        ],
        compiler_params=pltpu.CompilerParams(vmem_limit_bytes=SMALL),
        name="packed",
    )(*map(in_hbm, (tokens, norm_gain[None, :], expert_ids.T, gate_weights.T)))


def found_kernel(owner_ref, mine_ref):
    me = lax.axis_index("tok")
    mine_ref[0] = lax.fori_loop(
        0, owner_ref.shape[0], lambda i, found: jnp.where(owner_ref[i] == me, i, found), 0
    )


def loaded_kernel(count, *refs):
    sources, targets, sems = refs[:count], refs[count : 2 * count], refs[-1]
    moves = [
        pltpu.make_async_copy(source, target, sems.at[i])
        for i, (source, target) in enumerate(zip(sources, targets))
    ]
    for move in moves:
        move.start()
    for move in moves:
        move.wait()


def loaded(*arrays):
    count = len(arrays)
    return pl.pallas_call(
        functools.partial(loaded_kernel, count),
        out_shape=tuple(jax.ShapeDtypeStruct(x.shape, x.dtype) for x in arrays),
        in_specs=[pl.BlockSpec(memory_space=pltpu.HBM)] * count,
        out_specs=(pl.BlockSpec(memory_space=pltpu.VMEM),) * count,
        scratch_shapes=[pltpu.SemaphoreType.DMA((count,))],
        compiler_params=pltpu.CompilerParams(vmem_limit_bytes=SMALL),
        cost_estimate=pl.CostEstimate(
            flops=0, bytes_accessed=2 * sum(x.size for x in arrays), transcendentals=0
        ),
        name="loaded",
    )(*map(in_hbm, arrays))


def visit_kernel(
    experts, mine_ref, near_ref, far_ref, in_ref, in_scale_ref, down_ref, down_scale_ref,
    part_ref, lent_ref, rows_ref, hidden_ref,
):
    tok_rows, model_width = part_ref.shape
    hidden_width = hidden_ref.shape[1]
    rows_ref[:tok_rows] = near_ref[:, :model_width]
    rows_ref[tok_rows:] = far_ref[:, :model_width]
    rows = rows_ref[...]
    for start in range(0, hidden_width, TILE):
        cols = slice(start, start + TILE)
        gate = jnp.dot(rows, in_ref[0, 0, :, cols], preferred_element_type=jnp.float32)
        up = jnp.dot(rows, in_ref[0, 1, :, cols], preferred_element_type=jnp.float32)
        gate = gate * in_scale_ref[0, 0:1, cols].astype(jnp.float32)
        up = up * in_scale_ref[0, 1:2, cols].astype(jnp.float32)
        hidden_ref[:, cols] = (gate / (1.0 + jnp.exp(-gate)) * up).astype(jnp.bfloat16)
    lane = lax.broadcasted_iota(jnp.int32, (tok_rows, far_ref.shape[1] - model_width), 1)
    chosen = (lane == mine_ref[0]) | (lane == mine_ref[0] + experts)
    near = near_ref[:, model_width:].astype(jnp.float32)
    far = far_ref[:, model_width:].astype(jnp.float32)
    near_share = jnp.sum(jnp.where(chosen, near, 0.0), axis=1, keepdims=True)
    far_share = jnp.sum(jnp.where(chosen, far, 0.0), axis=1, keepdims=True)
    hidden = hidden_ref[...]
    for start in range(0, model_width, TILE):
        cols = slice(start, start + TILE)
        out = jnp.dot(hidden, down_ref[0, :, cols], preferred_element_type=jnp.float32)
        out = out * down_scale_ref[:, cols].astype(jnp.float32)
        part_ref[:, cols] = out[:tok_rows] * near_share
        lent_ref[:, cols] = (out[tok_rows:] * far_share).astype(jnp.bfloat16)


def visit(my_expert, near, far, experts, in_q, in_scale, down_q, down_scale):
    tok_rows = near.shape[0]
    hidden_width, model_width = down_q.shape[1:]
    flops = 2 * 2 * tok_rows * 3 * hidden_width * model_width
    return pl.pallas_call(
        functools.partial(visit_kernel, experts),
        out_shape=(
            jax.ShapeDtypeStruct((tok_rows, model_width), jnp.float32),
            jax.ShapeDtypeStruct((tok_rows, model_width), jnp.bfloat16),
        ),
        in_specs=[pl.BlockSpec(memory_space=pltpu.SMEM)]
        + [pl.BlockSpec(memory_space=pltpu.VMEM)] * 6,
        out_specs=(pl.BlockSpec(memory_space=pltpu.VMEM),) * 2,
        scratch_shapes=[
            pltpu.VMEM((2 * tok_rows, model_width), jnp.bfloat16),
            pltpu.VMEM((2 * tok_rows, hidden_width), jnp.bfloat16),
        ],
        compiler_params=pltpu.CompilerParams(vmem_limit_bytes=LARGE),
        cost_estimate=pl.CostEstimate(
            flops=flops, bytes_accessed=6 * tok_rows * model_width, transcendentals=0
        ),
        name="visit",
    )(my_expert, near, far, in_q, in_scale, down_q, down_scale)


def circulated(
    tokens, norm_gain, expert_ids, gate_weights, owner_map, in_q, in_scale, down_q, down_scale
):
    experts = owner_map.shape[0]
    devices = lax.axis_size("tok")
    ring, chips = ring_pairs(devices)
    swap = [(i, i ^ 1) for i in range(devices)]
    cut = tokens.shape[0] // 16 * 7
    block = packed(tokens, norm_gain, expert_ids, gate_weights, experts)
    blocks = loaded(in_q, in_scale, down_q, down_scale)
    mine = pl.pallas_call(
        found_kernel,
        out_shape=jax.ShapeDtypeStruct((1,), jnp.int32),
        in_specs=[pl.BlockSpec(memory_space=pltpu.SMEM)],
        out_specs=pl.BlockSpec(memory_space=pltpu.SMEM),
        compiler_params=pltpu.CompilerParams(vmem_limit_bytes=SMALL),
        name="found",
    )(owner_map)

    back = lax.ppermute(block, "tok", [(target, source) for source, target in ring])
    parts = []
    for step in range(chips):
        here = block if step < chips - 1 else back
        other = lax.ppermute(here, "tok", swap)
        if step < chips - 2:
            block = lax.ppermute(here, "tok", ring)
        part, lent = visit(mine, here, other, experts, *blocks)
        parts.append((part, lax.ppermute(lent, "tok", swap)))

    def summed(step, rows, arrived):
        part, lent = (x[rows].astype(jnp.float32) for x in parts[step])
        return (part + lent + arrived.astype(jnp.float32)).astype(jnp.bfloat16)

    total = jnp.zeros((), jnp.bfloat16)
    for step in range(1, chips - 2):
        total = lax.ppermute(summed(step, slice(None), total), "tok", ring)
    shares = {"a": slice(0, cut), "b": slice(cut, None)}
    totals = {name: total[rows] for name, rows in shares.items()}
    for step in range(chips - 2, chips):
        for name, rows in shares.items():
            totals[name] = lax.ppermute(summed(step, rows, totals[name]), "tok", ring)
    return jnp.concatenate([summed(0, rows, totals[name]) for name, rows in shares.items()])


def solution(mesh):
    devices = mesh.shape["tok"]
    row = P(("grp", "tok"), None)
    slot = [P("tok", *(None,) * extra) for extra in (3, 2, 2, 1)]

    def placed(body):
        return jax.shard_map(
            body,
            mesh=mesh,
            in_specs=(row, P(), row, row, P(), *slot),
            out_specs=row,
            check_vma=False,
        )

    def step(tokens, norm_gain, expert_ids, gate_weights, owner_map, *blocks):
        tok_rows = tokens.shape[0] // mesh.size
        experts = owner_map.shape[0]
        mean_load = tok_rows * expert_ids.shape[1] // experts
        routed = experts * (mean_load + mean_load // 2)
        arguments = (tokens, norm_gain, expert_ids, gate_weights, owner_map, *blocks)
        if tok_rows * devices > 2 * routed or devices % 4:
            return placed(exchanged)(*arguments)
        return placed(circulated)(*arguments)

    return step
```

```python
import functools

import jax
import jax.numpy as jnp
from jax import lax
from jax.experimental import pallas as pl
from jax.experimental.pallas import tpu as pltpu
from jax.sharding import PartitionSpec as P


LANES = 128
TALL = 16
TILE = 256
SMALL = 8 << 20
LARGE = 20 << 20


def expert_rows(batch_rows, in_blocks, in_scales, down_block, down_scales):
    gate_part = jnp.dot(batch_rows, in_blocks[0], preferred_element_type=jnp.float32) * in_scales[0]
    up_part = jnp.dot(batch_rows, in_blocks[1], preferred_element_type=jnp.float32) * in_scales[1]
    hidden = (jax.nn.silu(gate_part) * up_part).astype(jnp.bfloat16)
    return jnp.dot(hidden, down_block, preferred_element_type=jnp.float32) * down_scales


def normalized(tokens, norm_gain):
    values = tokens.astype(jnp.float32)
    row_scale = lax.rsqrt(jnp.mean(values * values, axis=1, keepdims=True) + 1e-06)
    return (values * row_scale * norm_gain).astype(jnp.bfloat16)


def exchanged(
    tokens, norm_gain, expert_ids, gate_weights, owner_map, in_q, in_scale, down_q, down_scale
):
    tok_rows, model_width = tokens.shape
    top_count = expert_ids.shape[1]
    experts = owner_map.shape[0]
    mean_load = tok_rows * top_count // experts
    capacity = mean_load + mean_load // 2
    normed = normalized(tokens, norm_gain)
    weights = gate_weights / jnp.sum(gate_weights, axis=1, keepdims=True)
    labels = jnp.arange(experts, dtype=jnp.int32)
    slot_table = jnp.sum(jnp.where(expert_ids[:, :, None] == labels, owner_map, 0), axis=2)
    flat_slot = slot_table.reshape(-1)
    onehot = (flat_slot[:, None] == labels).astype(jnp.int32)
    slot_rank = jnp.sum((jnp.cumsum(onehot, axis=0) - onehot) * onehot, axis=1)
    repeated = jnp.repeat(normed, top_count, axis=0)
    outgoing = (
        jnp.zeros((experts, capacity, model_width), jnp.bfloat16)
        .at[flat_slot, slot_rank]
        .set(repeated)
    )
    received = lax.all_to_all(outgoing, "tok", split_axis=0, concat_axis=0, tiled=True)
    source_count, slot_count, _ = received.shape
    flat_rows = received.reshape(source_count * slot_count, model_width)
    served = expert_rows(flat_rows, in_q[0], in_scale[0], down_q[0], down_scale[0])
    served = served.astype(jnp.bfloat16).reshape(source_count, slot_count, model_width)
    returned_rows = lax.all_to_all(served, "tok", split_axis=0, concat_axis=0, tiled=True)
    picked = returned_rows[flat_slot, slot_rank].reshape(tok_rows, top_count, model_width)
    mixed = jnp.sum(weights[:, :, None] * picked.astype(jnp.float32), axis=1)
    return mixed.astype(jnp.bfloat16)


def ring_pairs(devices):
    chips = devices // 2
    loop = list(range(0, chips, 2)) + list(range(chips - 1, 0, -2))
    pairs = []
    for place, chip in enumerate(loop):
        after = loop[(place + 1) % chips]
        pairs.append((2 * chip, 2 * after))
        pairs.append((2 * after + 1, 2 * chip + 1))
    return pairs, chips


def in_hbm(array):
    return pltpu.with_memory_space_constraint(array, pltpu.HBM)


def packed_kernel(tokens_hbm, gain_hbm, ids_hbm, gates_hbm, *refs):
    *part_refs, tokens, gain, ids, gates, sems = refs
    moves = [
        pltpu.make_async_copy(source, target, sems.at[i])
        for i, (source, target) in enumerate(
            ((ids_hbm, ids), (gates_hbm, gates), (tokens_hbm, tokens), (gain_hbm, gain))
        )
    ]
    for move in moves:
        move.start()
    tok_rows, model_width = tokens.shape
    moves[0].wait()
    moves[1].wait()
    weights = gates[...] / jnp.sum(gates[...], axis=0, keepdims=True)
    experts = (sum(ref.shape[0] for ref in part_refs) - tok_rows * model_width // LANES) // 2
    label = lax.broadcasted_iota(jnp.int32, (experts, tok_rows), 0)
    table = jnp.zeros((experts, tok_rows), jnp.float32)
    for k in range(ids.shape[0]):
        table += jnp.where(label == ids[k : k + 1, :], weights[k : k + 1, :], 0.0)
    high = table.astype(jnp.bfloat16)
    low = (table - high.astype(jnp.float32)).astype(jnp.bfloat16)
    last = part_refs[-1]
    last[-2 * experts : -experts, :] = high
    last[-experts:, :] = low
    moves[2].wait()
    moves[3].wait()
    places = tiles_of(part_refs, tok_rows, model_width)
    for top in range(0, tok_rows, TALL):
        values = tokens[top : top + TALL, :].astype(jnp.float32)
        row_scale = lax.rsqrt(jnp.mean(values * values, axis=1, keepdims=True) + 1e-06)
        normed = (values * row_scale * gain[...]).astype(jnp.bfloat16)
        for side in range(0, model_width, LANES):
            ref, row = places[top, side]
            ref[row : row + TALL, :] = normed[:, side : side + LANES]


def tiles_of(part_refs, tok_rows, model_width):
    tiles = [(top, side) for top in range(0, tok_rows, TALL) for side in range(0, model_width, LANES)]
    places, part, row = {}, 0, 0
    for tile in tiles:
        if row == part_refs[part].shape[0]:
            part, row = part + 1, 0
        places[tile] = part_refs[part], row
        row += TALL
    return places


def packed(tokens, norm_gain, expert_ids, gate_weights, experts):
    tok_rows, model_width = tokens.shape
    top_count = expert_ids.shape[1]
    size = tok_rows * model_width // LANES + 2 * experts
    return pl.pallas_call(
        packed_kernel,
        out_shape=(jax.ShapeDtypeStruct((size, LANES), jnp.bfloat16),),
        in_specs=[pl.BlockSpec(memory_space=pltpu.HBM)] * 4,
        out_specs=(pl.BlockSpec(memory_space=pltpu.VMEM),),
        scratch_shapes=[
            pltpu.VMEM((tok_rows, model_width), jnp.bfloat16),
            pltpu.VMEM((1, model_width), jnp.float32),
            pltpu.VMEM((top_count, tok_rows), jnp.int32),
            pltpu.VMEM((top_count, tok_rows), jnp.float32),
            pltpu.SemaphoreType.DMA((4,)),
        ],
        compiler_params=pltpu.CompilerParams(vmem_limit_bytes=SMALL),
        name="packed",
    )(*map(in_hbm, (tokens, norm_gain[None, :], expert_ids.T, gate_weights.T)))


def loaded_kernel(count, *refs):
    sources, targets, sems = refs[:count], refs[count : 2 * count], refs[-1]
    moves = [
        pltpu.make_async_copy(source, target, sems.at[i])
        for i, (source, target) in enumerate(zip(sources, targets))
    ]
    for move in moves:
        move.start()
    for move in moves:
        move.wait()


def loaded(*arrays):
    count = len(arrays)
    return pl.pallas_call(
        functools.partial(loaded_kernel, count),
        out_shape=tuple(jax.ShapeDtypeStruct(x.shape, x.dtype) for x in arrays),
        in_specs=[pl.BlockSpec(memory_space=pltpu.HBM)] * count,
        out_specs=(pl.BlockSpec(memory_space=pltpu.VMEM),) * count,
        scratch_shapes=[pltpu.SemaphoreType.DMA((count,))],
        compiler_params=pltpu.CompilerParams(vmem_limit_bytes=SMALL),
        cost_estimate=pl.CostEstimate(
            flops=0, bytes_accessed=2 * sum(x.size for x in arrays), transcendentals=0
        ),
        name="loaded",
    )(*map(in_hbm, arrays))


def visit_kernel(counts, owners_ref, *refs):
    near_refs, refs = refs[: counts[0]], refs[counts[0] :]
    far_refs, refs = refs[: counts[1]], refs[counts[1] :]
    in_ref, in_scale_ref, down_ref, down_scale_ref, part_ref, lent_ref, rows_ref, hidden_ref = refs
    tok_rows, model_width = part_ref.shape
    hidden_width = hidden_ref.shape[1]
    for base, block_refs in ((0, near_refs), (tok_rows, far_refs)):
        for (top, side), (ref, row) in tiles_of(block_refs, tok_rows, model_width).items():
            tile = ref[row : row + TALL, :]
            rows_ref[base + top : base + top + TALL, side : side + LANES] = tile
    rows = rows_ref[...]
    for start in range(0, hidden_width, TILE):
        cols = slice(start, start + TILE)
        gate = jnp.dot(rows, in_ref[0, 0, :, cols], preferred_element_type=jnp.float32)
        up = jnp.dot(rows, in_ref[0, 1, :, cols], preferred_element_type=jnp.float32)
        gate = gate * in_scale_ref[0, 0:1, cols].astype(jnp.float32)
        up = up * in_scale_ref[0, 1:2, cols].astype(jnp.float32)
        hidden_ref[:, cols] = (gate / (1.0 + jnp.exp(-gate)) * up).astype(jnp.bfloat16)
    experts = owners_ref.shape[1]
    lane = lax.broadcasted_iota(jnp.int32, owners_ref.shape, 1)
    here = owners_ref[...] == lax.axis_index("tok")
    mine = jnp.sum(jnp.where(here, lane, 0), axis=1, keepdims=True)
    label = lax.broadcasted_iota(jnp.int32, (2 * experts, tok_rows), 0)
    chosen = (label == mine) | (label == mine + experts)
    square = (tok_rows, tok_rows)
    same = lax.broadcasted_iota(jnp.int32, square, 0) == lax.broadcasted_iota(jnp.int32, square, 1)

    def share_of(block_refs):
        table = block_refs[-1][-2 * experts :, :].astype(jnp.float32)
        along = jnp.sum(jnp.where(chosen, table, 0.0), axis=0, keepdims=True)
        return jnp.sum(jnp.where(same, along, 0.0), axis=1, keepdims=True)

    near_share, far_share = share_of(near_refs), share_of(far_refs)
    hidden = hidden_ref[...]
    for start in range(0, model_width, TILE):
        cols = slice(start, start + TILE)
        out = jnp.dot(hidden, down_ref[0, :, cols], preferred_element_type=jnp.float32)
        out = out * down_scale_ref[:, cols].astype(jnp.float32)
        part_ref[:, cols] = out[:tok_rows] * near_share
        lent_ref[:, cols] = (out[tok_rows:] * far_share).astype(jnp.bfloat16)


def visit(near, far, owners, in_q, in_scale, down_q, down_scale):
    hidden_width, model_width = down_q.shape[1:]
    tok_rows = (sum(x.shape[0] for x in near) - 2 * owners.shape[1]) * LANES // model_width
    flops = 2 * 2 * tok_rows * 3 * hidden_width * model_width
    operands = (owners, *near, *far, in_q, in_scale, down_q, down_scale)
    return pl.pallas_call(
        functools.partial(visit_kernel, (len(near), len(far))),
        out_shape=(
            jax.ShapeDtypeStruct((tok_rows, model_width), jnp.float32),
            jax.ShapeDtypeStruct((tok_rows, model_width), jnp.bfloat16),
        ),
        in_specs=[pl.BlockSpec(memory_space=pltpu.VMEM)] * len(operands),
        out_specs=(pl.BlockSpec(memory_space=pltpu.VMEM),) * 2,
        scratch_shapes=[
            pltpu.VMEM((2 * tok_rows, model_width), jnp.bfloat16),
            pltpu.VMEM((2 * tok_rows, hidden_width), jnp.bfloat16),
        ],
        compiler_params=pltpu.CompilerParams(vmem_limit_bytes=LARGE),
        cost_estimate=pl.CostEstimate(
            flops=flops, bytes_accessed=6 * tok_rows * model_width, transcendentals=0
        ),
        name="visit",
    )(*operands)


def circulated(
    tokens, norm_gain, expert_ids, gate_weights, owner_map, in_q, in_scale, down_q, down_scale
):
    experts = owner_map.shape[0]
    devices = lax.axis_size("tok")
    ring, chips = ring_pairs(devices)
    swap = [(i, i ^ 1) for i in range(devices)]

    def moved(value, pairs):
        return lax.ppermute(value, "tok", pairs)

    (block,) = packed(tokens, norm_gain, expert_ids, gate_weights, experts)
    blocks = loaded(owner_map[None, :], in_q, in_scale, down_q, down_scale)
    back = moved(block, [(target, source) for source, target in ring])
    parts = []
    for step in range(chips):
        here = block if step < chips - 1 else back
        other = moved(here, swap)
        if step < chips - 2:
            block = moved(block, ring)
        part, lent = visit((here,), (other,), *blocks)
        parts.append((part, moved(lent, swap)))

    def summed(step, rows, arrived):
        part, lent = (x[rows].astype(jnp.float32) for x in parts[step])
        return (part + lent + arrived.astype(jnp.float32)).astype(jnp.bfloat16)

    total = jnp.zeros((), jnp.bfloat16)
    for step in range(1, chips - 2):
        total = lax.ppermute(summed(step, slice(None), total), "tok", ring)
    shares = shares_of(tokens.shape[0])
    totals = {name: total[rows] for name, rows in shares.items()}
    for step in range(chips - 2, chips):
        for name, rows in shares.items():
            totals[name] = lax.ppermute(summed(step, rows, totals[name]), "tok", ring)
    out = []
    for name, rows in shares.items():
        out.append(summed(0, rows, totals[name]))
    return jnp.concatenate(out)


def shares_of(tok_rows):
    one, two = tok_rows // 16 * 6, tok_rows // 16 * 9
    return {"a": slice(0, one), "b": slice(one, two), "c": slice(two, tok_rows)}


def solution(mesh):
    devices = mesh.shape["tok"]
    row = P(("grp", "tok"), None)
    slot = [P("tok", *(None,) * extra) for extra in (3, 2, 2, 1)]

    def placed(body):
        return jax.shard_map(
            body,
            mesh=mesh,
            in_specs=(row, P(), row, row, P(), *slot),
            out_specs=row,
            check_vma=False,
        )

    def step(tokens, norm_gain, expert_ids, gate_weights, owner_map, *blocks):
        tok_rows = tokens.shape[0] // mesh.size
        experts = owner_map.shape[0]
        mean_load = tok_rows * expert_ids.shape[1] // experts
        routed = experts * (mean_load + mean_load // 2)
        arguments = (tokens, norm_gain, expert_ids, gate_weights, owner_map, *blocks)
        if tok_rows * devices > 2 * routed or devices < 16 or devices % 4 or tok_rows != LANES:
            return placed(exchanged)(*arguments)
        return placed(circulated)(*arguments)

    return step
```

```python
import functools

import jax
import jax.numpy as jnp
from jax import lax
from jax.experimental import pallas as pl
from jax.experimental.pallas import tpu as pltpu
from jax.sharding import PartitionSpec as P


LANES = 128
TALL = 16
TILE = 256
SMALL = 8 << 20
LARGE = 20 << 20


def expert_rows(batch_rows, in_blocks, in_scales, down_block, down_scales):
    gate_part = jnp.dot(batch_rows, in_blocks[0], preferred_element_type=jnp.float32) * in_scales[0]
    up_part = jnp.dot(batch_rows, in_blocks[1], preferred_element_type=jnp.float32) * in_scales[1]
    hidden = (jax.nn.silu(gate_part) * up_part).astype(jnp.bfloat16)
    return jnp.dot(hidden, down_block, preferred_element_type=jnp.float32) * down_scales


def normalized(tokens, norm_gain):
    values = tokens.astype(jnp.float32)
    row_scale = lax.rsqrt(jnp.mean(values * values, axis=1, keepdims=True) + 1e-06)
    return (values * row_scale * norm_gain).astype(jnp.bfloat16)


def exchanged(
    tokens, norm_gain, expert_ids, gate_weights, owner_map, in_q, in_scale, down_q, down_scale
):
    tok_rows, model_width = tokens.shape
    top_count = expert_ids.shape[1]
    experts = owner_map.shape[0]
    mean_load = tok_rows * top_count // experts
    capacity = mean_load + mean_load // 2
    normed = normalized(tokens, norm_gain)
    weights = gate_weights / jnp.sum(gate_weights, axis=1, keepdims=True)
    labels = jnp.arange(experts, dtype=jnp.int32)
    slot_table = jnp.sum(jnp.where(expert_ids[:, :, None] == labels, owner_map, 0), axis=2)
    flat_slot = slot_table.reshape(-1)
    onehot = (flat_slot[:, None] == labels).astype(jnp.int32)
    slot_rank = jnp.sum((jnp.cumsum(onehot, axis=0) - onehot) * onehot, axis=1)
    repeated = jnp.repeat(normed, top_count, axis=0)
    outgoing = (
        jnp.zeros((experts, capacity, model_width), jnp.bfloat16)
        .at[flat_slot, slot_rank]
        .set(repeated)
    )
    received = lax.all_to_all(outgoing, "tok", split_axis=0, concat_axis=0, tiled=True)
    source_count, slot_count, _ = received.shape
    flat_rows = received.reshape(source_count * slot_count, model_width)
    served = expert_rows(flat_rows, in_q[0], in_scale[0], down_q[0], down_scale[0])
    served = served.astype(jnp.bfloat16).reshape(source_count, slot_count, model_width)
    returned_rows = lax.all_to_all(served, "tok", split_axis=0, concat_axis=0, tiled=True)
    picked = returned_rows[flat_slot, slot_rank].reshape(tok_rows, top_count, model_width)
    mixed = jnp.sum(weights[:, :, None] * picked.astype(jnp.float32), axis=1)
    return mixed.astype(jnp.bfloat16)


def ring_pairs(devices):
    chips = devices // 2
    loop = list(range(0, chips, 2)) + list(range(chips - 1, 0, -2))
    pairs = []
    for place, chip in enumerate(loop):
        after = loop[(place + 1) % chips]
        pairs.append((2 * chip, 2 * after))
        pairs.append((2 * after + 1, 2 * chip + 1))
    return pairs, chips


def in_hbm(array):
    return pltpu.with_memory_space_constraint(array, pltpu.HBM)


def packed_kernel(tokens_hbm, gain_hbm, ids_hbm, gates_hbm, *refs):
    out_ref, tokens, gain, ids, gates, sems = refs
    moves = [
        pltpu.make_async_copy(source, target, sems.at[i])
        for i, (source, target) in enumerate(
            ((ids_hbm, ids), (gates_hbm, gates), (tokens_hbm, tokens), (gain_hbm, gain))
        )
    ]
    for move in moves:
        move.start()
    tok_rows, model_width = tokens.shape
    moves[0].wait()
    moves[1].wait()
    weights = gates[...] / jnp.sum(gates[...], axis=0, keepdims=True)
    experts = (out_ref.shape[0] - tok_rows * model_width // LANES) // 2
    label = lax.broadcasted_iota(jnp.int32, (experts, tok_rows), 0)
    table = jnp.zeros((experts, tok_rows), jnp.float32)
    for k in range(ids.shape[0]):
        table += jnp.where(label == ids[k : k + 1, :], weights[k : k + 1, :], 0.0)
    high = table.astype(jnp.bfloat16)
    low = (table - high.astype(jnp.float32)).astype(jnp.bfloat16)
    out_ref[-2 * experts : -experts, :] = high
    out_ref[-experts:, :] = low
    moves[2].wait()
    moves[3].wait()
    for top in range(0, tok_rows, TALL):
        values = tokens[top : top + TALL, :].astype(jnp.float32)
        row_scale = lax.rsqrt(jnp.mean(values * values, axis=1, keepdims=True) + 1e-06)
        normed = (values * row_scale * gain[...]).astype(jnp.bfloat16)
        for side in range(0, model_width, LANES):
            row = top * model_width // LANES + side // LANES * TALL
            out_ref[row : row + TALL, :] = normed[:, side : side + LANES]


def packed(tokens, norm_gain, expert_ids, gate_weights, experts):
    tok_rows, model_width = tokens.shape
    top_count = expert_ids.shape[1]
    size = tok_rows * model_width // LANES + 2 * experts
    return pl.pallas_call(
        packed_kernel,
        out_shape=jax.ShapeDtypeStruct((size, LANES), jnp.bfloat16),
        in_specs=[pl.BlockSpec(memory_space=pltpu.HBM)] * 4,
        out_specs=pl.BlockSpec(memory_space=pltpu.VMEM),
        scratch_shapes=[
            pltpu.VMEM((tok_rows, model_width), jnp.bfloat16),
            pltpu.VMEM((1, model_width), jnp.float32),
            pltpu.VMEM((top_count, tok_rows), jnp.int32),
            pltpu.VMEM((top_count, tok_rows), jnp.float32),
            pltpu.SemaphoreType.DMA((4,)),
        ],
        compiler_params=pltpu.CompilerParams(vmem_limit_bytes=SMALL),
        name="packed",
    )(*map(in_hbm, (tokens, norm_gain[None, :], expert_ids.T, gate_weights.T)))


def loaded_kernel(count, *refs):
    sources, targets, sems = refs[:count], refs[count : 2 * count], refs[-1]
    moves = [
        pltpu.make_async_copy(source, target, sems.at[i])
        for i, (source, target) in enumerate(zip(sources, targets))
    ]
    for move in moves:
        move.start()
    for move in moves:
        move.wait()


def loaded(*arrays):
    count = len(arrays)
    return pl.pallas_call(
        functools.partial(loaded_kernel, count),
        out_shape=tuple(jax.ShapeDtypeStruct(x.shape, x.dtype) for x in arrays),
        in_specs=[pl.BlockSpec(memory_space=pltpu.HBM)] * count,
        out_specs=(pl.BlockSpec(memory_space=pltpu.VMEM),) * count,
        scratch_shapes=[pltpu.SemaphoreType.DMA((count,))],
        compiler_params=pltpu.CompilerParams(vmem_limit_bytes=SMALL),
        cost_estimate=pl.CostEstimate(
            flops=0, bytes_accessed=2 * sum(x.size for x in arrays), transcendentals=0
        ),
        name="loaded",
    )(*map(in_hbm, arrays))


def visit_kernel(count, owners_ref, *refs):
    block_refs, refs = refs[:count], refs[count:]
    in_ref, in_scale_ref, down_ref, down_scale_ref = refs[:4]
    out_refs, (rows_ref, hidden_ref) = refs[4 : 4 + count], refs[4 + count :]
    tok_rows, model_width = out_refs[0].shape
    hidden_width = hidden_ref.shape[1]
    tall = [(top, side) for top in range(0, tok_rows, TALL) for side in range(0, model_width, LANES)]
    for i, block_ref in enumerate(block_refs):
        for place, (top, side) in enumerate(tall):
            tile = block_ref[place * TALL : (place + 1) * TALL, :]
            base = i * tok_rows + top
            rows_ref[base : base + TALL, side : side + LANES] = tile
    rows = rows_ref[...]
    for start in range(0, hidden_width, TILE):
        cols = slice(start, start + TILE)
        gate = jnp.dot(rows, in_ref[0, 0, :, cols], preferred_element_type=jnp.float32)
        up = jnp.dot(rows, in_ref[0, 1, :, cols], preferred_element_type=jnp.float32)
        gate = gate * in_scale_ref[0, 0:1, cols].astype(jnp.float32)
        up = up * in_scale_ref[0, 1:2, cols].astype(jnp.float32)
        hidden_ref[:, cols] = (gate / (1.0 + jnp.exp(-gate)) * up).astype(jnp.bfloat16)
    experts = owners_ref.shape[1]
    lane = lax.broadcasted_iota(jnp.int32, owners_ref.shape, 1)
    here = owners_ref[...] == lax.axis_index("tok")
    mine = jnp.sum(jnp.where(here, lane, 0), axis=1, keepdims=True)
    label = lax.broadcasted_iota(jnp.int32, (2 * experts, tok_rows), 0)
    chosen = (label == mine) | (label == mine + experts)
    square = (tok_rows, tok_rows)
    same = lax.broadcasted_iota(jnp.int32, square, 0) == lax.broadcasted_iota(jnp.int32, square, 1)
    shares = []
    for block_ref in block_refs:
        table = block_ref[-2 * experts :, :].astype(jnp.float32)
        along = jnp.sum(jnp.where(chosen, table, 0.0), axis=0, keepdims=True)
        shares.append(jnp.sum(jnp.where(same, along, 0.0), axis=1, keepdims=True))
    hidden = hidden_ref[...]
    for start in range(0, model_width, TILE):
        cols = slice(start, start + TILE)
        out = jnp.dot(hidden, down_ref[0, :, cols], preferred_element_type=jnp.float32)
        out = out * down_scale_ref[:, cols].astype(jnp.float32)
        for i, (out_ref, share) in enumerate(zip(out_refs, shares)):
            weighted = out[i * tok_rows : (i + 1) * tok_rows] * share
            out_ref[:, cols] = weighted.astype(out_ref.dtype)


def visit(visitors, kinds, owners, in_q, in_scale, down_q, down_scale):
    hidden_width, model_width = down_q.shape[1:]
    tok_rows = (visitors[0].shape[0] - 2 * owners.shape[1]) * LANES // model_width
    count = len(visitors)
    operands = (owners, *visitors, in_q, in_scale, down_q, down_scale)
    return pl.pallas_call(
        functools.partial(visit_kernel, count),
        out_shape=tuple(jax.ShapeDtypeStruct((tok_rows, model_width), kind) for kind in kinds),
        in_specs=[pl.BlockSpec(memory_space=pltpu.VMEM)] * len(operands),
        out_specs=(pl.BlockSpec(memory_space=pltpu.VMEM),) * count,
        scratch_shapes=[
            pltpu.VMEM((count * tok_rows, model_width), jnp.bfloat16),
            pltpu.VMEM((count * tok_rows, hidden_width), jnp.bfloat16),
        ],
        compiler_params=pltpu.CompilerParams(vmem_limit_bytes=LARGE),
        cost_estimate=pl.CostEstimate(
            flops=2 * count * tok_rows * 3 * hidden_width * model_width,
            bytes_accessed=3 * count * tok_rows * model_width,
            transcendentals=0,
        ),
        name="visit",
    )(*operands)


def circulated(
    tokens, norm_gain, expert_ids, gate_weights, owner_map, in_q, in_scale, down_q, down_scale
):
    experts = owner_map.shape[0]
    devices = lax.axis_size("tok")
    ring, chips = ring_pairs(devices)
    swap = [(i, i ^ 1) for i in range(devices)]

    def moved(value, pairs):
        return lax.ppermute(value, "tok", pairs)

    block = packed(tokens, norm_gain, expert_ids, gate_weights, experts)
    blocks = loaded(owner_map[None, :], in_q, in_scale, down_q, down_scale)
    back = moved(block, [(target, source) for source, target in ring])
    parts = []
    for step in range(chips):
        here = block if step < chips - 1 else back
        other = moved(here, swap)
        if step < chips - 2:
            block = moved(block, ring)
        if step == chips - 2:
            (part,) = visit((here,), (jnp.float32,), *blocks)
            (lent,) = visit((other,), (jnp.bfloat16,), *blocks)
        else:
            part, lent = visit((here, other), (jnp.float32, jnp.bfloat16), *blocks)
        parts.append((part, moved(lent, swap)))

    def summed(step, rows, arrived):
        part, lent = (x[rows].astype(jnp.float32) for x in parts[step])
        return (part + lent + arrived.astype(jnp.float32)).astype(jnp.bfloat16)

    total = jnp.zeros((), jnp.bfloat16)
    for step in range(1, chips - 2):
        total = lax.ppermute(summed(step, slice(None), total), "tok", ring)
    shares = shares_of(tokens.shape[0])
    totals = {name: total[rows] for name, rows in shares.items()}
    for step in range(chips - 2, chips):
        for name, rows in shares.items():
            totals[name] = lax.ppermute(summed(step, rows, totals[name]), "tok", ring)
    out = []
    for name, rows in shares.items():
        out.append(summed(0, rows, totals[name]))
    return jnp.concatenate(out)


def shares_of(tok_rows):
    one, two = tok_rows // 16 * 7, tok_rows // 16 * 12
    return {"a": slice(0, one), "b": slice(one, two), "c": slice(two, tok_rows)}


def solution(mesh):
    devices = mesh.shape["tok"]
    row = P(("grp", "tok"), None)
    slot = [P("tok", *(None,) * extra) for extra in (3, 2, 2, 1)]

    def placed(body):
        return jax.shard_map(
            body,
            mesh=mesh,
            in_specs=(row, P(), row, row, P(), *slot),
            out_specs=row,
            check_vma=False,
        )

    def step(tokens, norm_gain, expert_ids, gate_weights, owner_map, *blocks):
        tok_rows = tokens.shape[0] // mesh.size
        experts = owner_map.shape[0]
        mean_load = tok_rows * expert_ids.shape[1] // experts
        routed = experts * (mean_load + mean_load // 2)
        arguments = (tokens, norm_gain, expert_ids, gate_weights, owner_map, *blocks)
        if tok_rows * devices > 2 * routed or devices < 16 or devices % 4 or tok_rows != LANES:
            return placed(exchanged)(*arguments)
        return placed(circulated)(*arguments)

    return step
```

```python
import functools

import jax
import jax.numpy as jnp
from jax import lax
from jax.experimental import pallas as pl
from jax.experimental.pallas import tpu as pltpu
from jax.sharding import PartitionSpec as P


LANES = 128
TALL = 16
TILE = 256
SMALL = 8 << 20
LARGE = 20 << 20


def expert_rows(batch_rows, in_blocks, in_scales, down_block, down_scales):
    gate_part = jnp.dot(batch_rows, in_blocks[0], preferred_element_type=jnp.float32) * in_scales[0]
    up_part = jnp.dot(batch_rows, in_blocks[1], preferred_element_type=jnp.float32) * in_scales[1]
    hidden = (jax.nn.silu(gate_part) * up_part).astype(jnp.bfloat16)
    return jnp.dot(hidden, down_block, preferred_element_type=jnp.float32) * down_scales


def normalized(tokens, norm_gain):
    values = tokens.astype(jnp.float32)
    row_scale = lax.rsqrt(jnp.mean(values * values, axis=1, keepdims=True) + 1e-06)
    return (values * row_scale * norm_gain).astype(jnp.bfloat16)


def exchanged(
    tokens, norm_gain, expert_ids, gate_weights, owner_map, in_q, in_scale, down_q, down_scale
):
    tok_rows, model_width = tokens.shape
    top_count = expert_ids.shape[1]
    experts = owner_map.shape[0]
    mean_load = tok_rows * top_count // experts
    capacity = mean_load + mean_load // 2
    normed = normalized(tokens, norm_gain)
    weights = gate_weights / jnp.sum(gate_weights, axis=1, keepdims=True)
    labels = jnp.arange(experts, dtype=jnp.int32)
    slot_table = jnp.sum(jnp.where(expert_ids[:, :, None] == labels, owner_map, 0), axis=2)
    flat_slot = slot_table.reshape(-1)
    onehot = (flat_slot[:, None] == labels).astype(jnp.int32)
    slot_rank = jnp.sum((jnp.cumsum(onehot, axis=0) - onehot) * onehot, axis=1)
    repeated = jnp.repeat(normed, top_count, axis=0)
    outgoing = (
        jnp.zeros((experts, capacity, model_width), jnp.bfloat16)
        .at[flat_slot, slot_rank]
        .set(repeated)
    )
    received = lax.all_to_all(outgoing, "tok", split_axis=0, concat_axis=0, tiled=True)
    source_count, slot_count, _ = received.shape
    flat_rows = received.reshape(source_count * slot_count, model_width)
    served = expert_rows(flat_rows, in_q[0], in_scale[0], down_q[0], down_scale[0])
    served = served.astype(jnp.bfloat16).reshape(source_count, slot_count, model_width)
    returned_rows = lax.all_to_all(served, "tok", split_axis=0, concat_axis=0, tiled=True)
    picked = returned_rows[flat_slot, slot_rank].reshape(tok_rows, top_count, model_width)
    mixed = jnp.sum(weights[:, :, None] * picked.astype(jnp.float32), axis=1)
    return mixed.astype(jnp.bfloat16)


def ring_pairs(devices):
    chips = devices // 2
    loop = list(range(0, chips, 2)) + list(range(chips - 1, 0, -2))
    pairs = []
    for place, chip in enumerate(loop):
        after = loop[(place + 1) % chips]
        pairs.append((2 * chip, 2 * after))
        pairs.append((2 * after + 1, 2 * chip + 1))
    return pairs, chips


def in_hbm(array):
    return pltpu.with_memory_space_constraint(array, pltpu.HBM)


def write_rows(tokens, gain, out_ref):
    tok_rows, model_width = tokens.shape
    for top in range(0, tok_rows, TALL):
        values = tokens[top : top + TALL, :].astype(jnp.float32)
        row_scale = lax.rsqrt(jnp.mean(values * values, axis=1, keepdims=True) + 1e-06)
        normed = (values * row_scale * gain[...]).astype(jnp.bfloat16)
        for side in range(0, model_width, LANES):
            row = top * model_width // LANES + side // LANES * TALL
            out_ref[row : row + TALL, :] = normed[:, side : side + LANES]


def packed_kernel(
    tokens_hbm, gain_hbm, ids_hbm, gates_hbm, out_ref, table_ref, tokens, gain, ids, gates, sems
):
    moves = [
        pltpu.make_async_copy(source, target, sems.at[i])
        for i, (source, target) in enumerate(
            ((ids_hbm, ids), (gates_hbm, gates), (tokens_hbm, tokens), (gain_hbm, gain))
        )
    ]
    for move in moves:
        move.start()
    moves[0].wait()
    moves[1].wait()
    weights = gates[...] / jnp.sum(gates[...], axis=0, keepdims=True)
    experts = table_ref.shape[0] // 2
    label = lax.broadcasted_iota(jnp.int32, (experts, tokens.shape[0]), 0)
    table = jnp.zeros(label.shape, jnp.float32)
    for k in range(ids.shape[0]):
        table += jnp.where(label == ids[k : k + 1, :], weights[k : k + 1, :], 0.0)
    high = table.astype(jnp.bfloat16)
    table_ref[:experts, :] = high
    table_ref[experts:, :] = (table - high.astype(jnp.float32)).astype(jnp.bfloat16)
    out_ref[-2 * experts :, :] = table_ref[...]
    moves[2].wait()
    moves[3].wait()
    write_rows(tokens, gain, out_ref)


def packed(tokens, norm_gain, expert_ids, gate_weights, experts):
    tok_rows, model_width = tokens.shape
    top_count = expert_ids.shape[1]
    size = tok_rows * model_width // LANES + 2 * experts
    return pl.pallas_call(
        packed_kernel,
        out_shape=tuple(
            jax.ShapeDtypeStruct((rows, LANES), jnp.bfloat16) for rows in (size, 2 * experts)
        ),
        in_specs=[pl.BlockSpec(memory_space=pltpu.HBM)] * 4,
        out_specs=(pl.BlockSpec(memory_space=pltpu.VMEM),) * 2,
        scratch_shapes=[
            pltpu.VMEM((tok_rows, model_width), jnp.bfloat16),
            pltpu.VMEM((1, model_width), jnp.float32),
            pltpu.VMEM((top_count, tok_rows), jnp.int32),
            pltpu.VMEM((top_count, tok_rows), jnp.float32),
            pltpu.SemaphoreType.DMA((4,)),
        ],
        compiler_params=pltpu.CompilerParams(vmem_limit_bytes=SMALL),
        name="packed",
    )(*map(in_hbm, (tokens, norm_gain[None, :], expert_ids.T, gate_weights.T)))


def mended_kernel(tokens_ref, table_ref, gain_ref, out_ref):
    out_ref[-table_ref.shape[0] :, :] = table_ref[...]
    write_rows(tokens_ref, gain_ref, out_ref)


def mended(tokens, table, gain):
    size = tokens.size // LANES + table.shape[0]
    return pl.pallas_call(
        mended_kernel,
        out_shape=jax.ShapeDtypeStruct((size, LANES), jnp.bfloat16),
        in_specs=[pl.BlockSpec(memory_space=pltpu.VMEM)] * 3,
        out_specs=pl.BlockSpec(memory_space=pltpu.VMEM),
        compiler_params=pltpu.CompilerParams(vmem_limit_bytes=SMALL),
        name="mended",
    )(tokens, table, gain)


def loaded_kernel(count, *refs):
    sources, targets, sems = refs[:count], refs[count : 2 * count], refs[-1]
    moves = [
        pltpu.make_async_copy(source, target, sems.at[i])
        for i, (source, target) in enumerate(zip(sources, targets))
    ]
    for move in moves:
        move.start()
    for move in moves:
        move.wait()


def loaded(*arrays):
    count = len(arrays)
    return pl.pallas_call(
        functools.partial(loaded_kernel, count),
        out_shape=tuple(jax.ShapeDtypeStruct(x.shape, x.dtype) for x in arrays),
        in_specs=[pl.BlockSpec(memory_space=pltpu.HBM)] * count,
        out_specs=(pl.BlockSpec(memory_space=pltpu.VMEM),) * count,
        scratch_shapes=[pltpu.SemaphoreType.DMA((count,))],
        compiler_params=pltpu.CompilerParams(vmem_limit_bytes=SMALL),
        cost_estimate=pl.CostEstimate(
            flops=0, bytes_accessed=2 * sum(x.size for x in arrays), transcendentals=0
        ),
        name="loaded",
    )(*map(in_hbm, arrays))


def visit_kernel(count, owners_ref, *refs):
    block_refs, refs = refs[:count], refs[count:]
    in_ref, in_scale_ref, down_ref, down_scale_ref = refs[:4]
    out_refs, (rows_ref, hidden_ref) = refs[4 : 4 + count], refs[4 + count :]
    tok_rows, model_width = out_refs[0].shape
    hidden_width = hidden_ref.shape[1]
    tall = [(top, side) for top in range(0, tok_rows, TALL) for side in range(0, model_width, LANES)]
    for i, block_ref in enumerate(block_refs):
        for place, (top, side) in enumerate(tall):
            tile = block_ref[place * TALL : (place + 1) * TALL, :]
            base = i * tok_rows + top
            rows_ref[base : base + TALL, side : side + LANES] = tile
    rows = rows_ref[...]
    for start in range(0, hidden_width, TILE):
        cols = slice(start, start + TILE)
        gate = jnp.dot(rows, in_ref[0, 0, :, cols], preferred_element_type=jnp.float32)
        up = jnp.dot(rows, in_ref[0, 1, :, cols], preferred_element_type=jnp.float32)
        gate = gate * in_scale_ref[0, 0:1, cols].astype(jnp.float32)
        up = up * in_scale_ref[0, 1:2, cols].astype(jnp.float32)
        hidden_ref[:, cols] = (gate / (1.0 + jnp.exp(-gate)) * up).astype(jnp.bfloat16)
    experts = owners_ref.shape[1]
    lane = lax.broadcasted_iota(jnp.int32, owners_ref.shape, 1)
    here = owners_ref[...] == lax.axis_index("tok")
    mine = jnp.sum(jnp.where(here, lane, 0), axis=1, keepdims=True)
    label = lax.broadcasted_iota(jnp.int32, (2 * experts, tok_rows), 0)
    chosen = (label == mine) | (label == mine + experts)
    square = (tok_rows, tok_rows)
    same = lax.broadcasted_iota(jnp.int32, square, 0) == lax.broadcasted_iota(jnp.int32, square, 1)
    shares = []
    for block_ref in block_refs:
        table = block_ref[-2 * experts :, :].astype(jnp.float32)
        along = jnp.sum(jnp.where(chosen, table, 0.0), axis=0, keepdims=True)
        shares.append(jnp.sum(jnp.where(same, along, 0.0), axis=1, keepdims=True))
    hidden = hidden_ref[...]
    for start in range(0, model_width, TILE):
        cols = slice(start, start + TILE)
        out = jnp.dot(hidden, down_ref[0, :, cols], preferred_element_type=jnp.float32)
        out = out * down_scale_ref[:, cols].astype(jnp.float32)
        for i, (out_ref, share) in enumerate(zip(out_refs, shares)):
            weighted = out[i * tok_rows : (i + 1) * tok_rows] * share
            out_ref[:, cols] = weighted.astype(out_ref.dtype)


def visit(visitors, kinds, owners, in_q, in_scale, down_q, down_scale):
    hidden_width, model_width = down_q.shape[1:]
    tok_rows = (visitors[0].shape[0] - 2 * owners.shape[1]) * LANES // model_width
    count = len(visitors)
    operands = (owners, *visitors, in_q, in_scale, down_q, down_scale)
    return pl.pallas_call(
        functools.partial(visit_kernel, count),
        out_shape=tuple(jax.ShapeDtypeStruct((tok_rows, model_width), kind) for kind in kinds),
        in_specs=[pl.BlockSpec(memory_space=pltpu.VMEM)] * len(operands),
        out_specs=(pl.BlockSpec(memory_space=pltpu.VMEM),) * count,
        scratch_shapes=[
            pltpu.VMEM((count * tok_rows, model_width), jnp.bfloat16),
            pltpu.VMEM((count * tok_rows, hidden_width), jnp.bfloat16),
        ],
        compiler_params=pltpu.CompilerParams(vmem_limit_bytes=LARGE),
        cost_estimate=pl.CostEstimate(
            flops=2 * count * tok_rows * 3 * hidden_width * model_width,
            bytes_accessed=3 * count * tok_rows * model_width,
            transcendentals=0,
        ),
        name="visit",
    )(*operands)


def circulated(
    tokens, norm_gain, expert_ids, gate_weights, owner_map, in_q, in_scale, down_q, down_scale
):
    experts = owner_map.shape[0]
    devices = lax.axis_size("tok")
    ring, chips = ring_pairs(devices)
    swap = [(i, i ^ 1) for i in range(devices)]

    def moved(value, pairs):
        return lax.ppermute(value, "tok", pairs)

    raw = moved(tokens, ring)
    block, table = packed(tokens, norm_gain, expert_ids, gate_weights, experts)
    table = moved(table, ring)
    gain, *blocks = loaded(
        norm_gain[None, :], owner_map[None, :], in_q, in_scale, down_q, down_scale
    )
    back = moved(block, [(target, source) for source, target in ring])
    near = mended(raw, table, gain)
    parts = []
    for step in range(chips):
        here = {0: block, chips - 1: back}.get(step, near)
        other = moved(here, swap)
        if 0 < step < chips - 2:
            near = moved(near, ring)
        if step == chips - 2:
            (part,) = visit((here,), (jnp.float32,), *blocks)
            (lent,) = visit((other,), (jnp.bfloat16,), *blocks)
        else:
            part, lent = visit((here, other), (jnp.float32, jnp.bfloat16), *blocks)
        parts.append((part, moved(lent, swap)))

    def summed(step, rows, arrived):
        part, lent = (x[rows].astype(jnp.float32) for x in parts[step])
        return (part + lent + arrived.astype(jnp.float32)).astype(jnp.bfloat16)

    total = jnp.zeros((), jnp.bfloat16)
    for step in range(1, chips - 2):
        total = lax.ppermute(summed(step, slice(None), total), "tok", ring)
    shares = shares_of(tokens.shape[0])
    totals = {name: total[rows] for name, rows in shares.items()}
    for step in range(chips - 2, chips):
        for name, rows in shares.items():
            totals[name] = lax.ppermute(summed(step, rows, totals[name]), "tok", ring)
    out = []
    for name, rows in shares.items():
        out.append(summed(0, rows, totals[name]))
    return jnp.concatenate(out)


def shares_of(tok_rows):
    one, two = tok_rows // 16 * 7, tok_rows // 16 * 12
    return {"a": slice(0, one), "b": slice(one, two), "c": slice(two, tok_rows)}


def solution(mesh):
    devices = mesh.shape["tok"]
    row = P(("grp", "tok"), None)
    slot = [P("tok", *(None,) * extra) for extra in (3, 2, 2, 1)]

    def placed(body):
        return jax.shard_map(
            body,
            mesh=mesh,
            in_specs=(row, P(), row, row, P(), *slot),
            out_specs=row,
            check_vma=False,
        )

    def step(tokens, norm_gain, expert_ids, gate_weights, owner_map, *blocks):
        tok_rows = tokens.shape[0] // mesh.size
        experts = owner_map.shape[0]
        mean_load = tok_rows * expert_ids.shape[1] // experts
        routed = experts * (mean_load + mean_load // 2)
        arguments = (tokens, norm_gain, expert_ids, gate_weights, owner_map, *blocks)
        if tok_rows * devices > 2 * routed or devices < 16 or devices % 4 or tok_rows != LANES:
            return placed(exchanged)(*arguments)
        return placed(circulated)(*arguments)

    return step
```

```python
import functools

import jax
import jax.numpy as jnp
from jax import lax
from jax.experimental import pallas as pl
from jax.experimental.pallas import tpu as pltpu
from jax.sharding import PartitionSpec as P


LANES = 128
TALL = 16
TILE = 256
SMALL = 8 << 20
LARGE = 20 << 20


def expert_rows(batch_rows, in_blocks, in_scales, down_block, down_scales):
    gate_part = jnp.dot(batch_rows, in_blocks[0], preferred_element_type=jnp.float32) * in_scales[0]
    up_part = jnp.dot(batch_rows, in_blocks[1], preferred_element_type=jnp.float32) * in_scales[1]
    hidden = (jax.nn.silu(gate_part) * up_part).astype(jnp.bfloat16)
    return jnp.dot(hidden, down_block, preferred_element_type=jnp.float32) * down_scales


def normalized(tokens, norm_gain):
    values = tokens.astype(jnp.float32)
    row_scale = lax.rsqrt(jnp.mean(values * values, axis=1, keepdims=True) + 1e-06)
    return (values * row_scale * norm_gain).astype(jnp.bfloat16)


def exchanged(
    tokens, norm_gain, expert_ids, gate_weights, owner_map, in_q, in_scale, down_q, down_scale
):
    tok_rows, model_width = tokens.shape
    top_count = expert_ids.shape[1]
    experts = owner_map.shape[0]
    mean_load = tok_rows * top_count // experts
    capacity = mean_load + mean_load // 2
    normed = normalized(tokens, norm_gain)
    weights = gate_weights / jnp.sum(gate_weights, axis=1, keepdims=True)
    labels = jnp.arange(experts, dtype=jnp.int32)
    slot_table = jnp.sum(jnp.where(expert_ids[:, :, None] == labels, owner_map, 0), axis=2)
    flat_slot = slot_table.reshape(-1)
    onehot = (flat_slot[:, None] == labels).astype(jnp.int32)
    slot_rank = jnp.sum((jnp.cumsum(onehot, axis=0) - onehot) * onehot, axis=1)
    repeated = jnp.repeat(normed, top_count, axis=0)
    outgoing = (
        jnp.zeros((experts, capacity, model_width), jnp.bfloat16)
        .at[flat_slot, slot_rank]
        .set(repeated)
    )
    received = lax.all_to_all(outgoing, "tok", split_axis=0, concat_axis=0, tiled=True)
    source_count, slot_count, _ = received.shape
    flat_rows = received.reshape(source_count * slot_count, model_width)
    served = expert_rows(flat_rows, in_q[0], in_scale[0], down_q[0], down_scale[0])
    served = served.astype(jnp.bfloat16).reshape(source_count, slot_count, model_width)
    returned_rows = lax.all_to_all(served, "tok", split_axis=0, concat_axis=0, tiled=True)
    picked = returned_rows[flat_slot, slot_rank].reshape(tok_rows, top_count, model_width)
    mixed = jnp.sum(weights[:, :, None] * picked.astype(jnp.float32), axis=1)
    return mixed.astype(jnp.bfloat16)


def ring_pairs(devices):
    chips = devices // 2
    loop = list(range(0, chips, 2)) + list(range(chips - 1, 0, -2))
    pairs = []
    for place, chip in enumerate(loop):
        after = loop[(place + 1) % chips]
        pairs.append((2 * chip, 2 * after))
        pairs.append((2 * after + 1, 2 * chip + 1))
    return pairs, chips


def in_hbm(array):
    return pltpu.with_memory_space_constraint(array, pltpu.HBM)


def write_rows(tokens, gain, out_ref):
    tok_rows, model_width = tokens.shape
    for top in range(0, tok_rows, TALL):
        values = tokens[top : top + TALL, :].astype(jnp.float32)
        row_scale = lax.rsqrt(jnp.mean(values * values, axis=1, keepdims=True) + 1e-06)
        normed = (values * row_scale * gain[...]).astype(jnp.bfloat16)
        for side in range(0, model_width, LANES):
            row = top * model_width // LANES + side // LANES * TALL
            out_ref[row : row + TALL, :] = normed[:, side : side + LANES]


def packed_kernel(
    tokens_hbm, gain_hbm, ids_hbm, gates_hbm, out_ref, table_ref, tokens, gain, ids, gates, sems
):
    moves = [
        pltpu.make_async_copy(source, target, sems.at[i])
        for i, (source, target) in enumerate(
            ((ids_hbm, ids), (gates_hbm, gates), (tokens_hbm, tokens), (gain_hbm, gain))
        )
    ]
    for move in moves:
        move.start()
    moves[0].wait()
    moves[1].wait()
    weights = gates[...] / jnp.sum(gates[...], axis=0, keepdims=True)
    experts = table_ref.shape[0] // 2
    label = lax.broadcasted_iota(jnp.int32, (experts, tokens.shape[0]), 0)
    table = jnp.zeros(label.shape, jnp.float32)
    for k in range(ids.shape[0]):
        table += jnp.where(label == ids[k : k + 1, :], weights[k : k + 1, :], 0.0)
    high = table.astype(jnp.bfloat16)
    table_ref[:experts, :] = high
    table_ref[experts:, :] = (table - high.astype(jnp.float32)).astype(jnp.bfloat16)
    out_ref[-2 * experts :, :] = table_ref[...]
    moves[2].wait()
    moves[3].wait()
    write_rows(tokens, gain, out_ref)


def packed(tokens, norm_gain, expert_ids, gate_weights, experts):
    tok_rows, model_width = tokens.shape
    top_count = expert_ids.shape[1]
    size = tok_rows * model_width // LANES + 2 * experts
    return pl.pallas_call(
        packed_kernel,
        out_shape=tuple(
            jax.ShapeDtypeStruct((rows, LANES), jnp.bfloat16) for rows in (size, 2 * experts)
        ),
        in_specs=[pl.BlockSpec(memory_space=pltpu.HBM)] * 4,
        out_specs=(pl.BlockSpec(memory_space=pltpu.VMEM),) * 2,
        scratch_shapes=[
            pltpu.VMEM((tok_rows, model_width), jnp.bfloat16),
            pltpu.VMEM((1, model_width), jnp.float32),
            pltpu.VMEM((top_count, tok_rows), jnp.int32),
            pltpu.VMEM((top_count, tok_rows), jnp.float32),
            pltpu.SemaphoreType.DMA((4,)),
        ],
        compiler_params=pltpu.CompilerParams(vmem_limit_bytes=SMALL),
        name="packed",
    )(*map(in_hbm, (tokens, norm_gain[None, :], expert_ids.T, gate_weights.T)))


def mended_kernel(tokens_ref, table_ref, gain_ref, out_ref):
    out_ref[-table_ref.shape[0] :, :] = table_ref[...]
    write_rows(tokens_ref, gain_ref, out_ref)


def mended(tokens, table, gain):
    size = tokens.size // LANES + table.shape[0]
    return pl.pallas_call(
        mended_kernel,
        out_shape=jax.ShapeDtypeStruct((size, LANES), jnp.bfloat16),
        in_specs=[pl.BlockSpec(memory_space=pltpu.VMEM)] * 3,
        out_specs=pl.BlockSpec(memory_space=pltpu.VMEM),
        compiler_params=pltpu.CompilerParams(vmem_limit_bytes=SMALL),
        name="mended",
    )(tokens, table, gain)


def loaded_kernel(count, *refs):
    sources, targets, sems = refs[:count], refs[count : 2 * count], refs[-1]
    moves = [
        pltpu.make_async_copy(source, target, sems.at[i])
        for i, (source, target) in enumerate(zip(sources, targets))
    ]
    for move in moves:
        move.start()
    for move in moves:
        move.wait()


def loaded(*arrays):
    count = len(arrays)
    return pl.pallas_call(
        functools.partial(loaded_kernel, count),
        out_shape=tuple(jax.ShapeDtypeStruct(x.shape, x.dtype) for x in arrays),
        in_specs=[pl.BlockSpec(memory_space=pltpu.HBM)] * count,
        out_specs=(pl.BlockSpec(memory_space=pltpu.VMEM),) * count,
        scratch_shapes=[pltpu.SemaphoreType.DMA((count,))],
        compiler_params=pltpu.CompilerParams(vmem_limit_bytes=SMALL),
        cost_estimate=pl.CostEstimate(
            flops=0, bytes_accessed=2 * sum(x.size for x in arrays), transcendentals=0
        ),
        name="loaded",
    )(*map(in_hbm, arrays))


def visit_kernel(count, owners_ref, *refs):
    block_refs, refs = refs[:count], refs[count:]
    in_ref, in_scale_ref, down_ref, down_scale_ref = refs[:4]
    out_refs, (rows_ref, hidden_ref) = refs[4 : 4 + count], refs[4 + count :]
    tok_rows, model_width = out_refs[0].shape
    hidden_width = hidden_ref.shape[1]
    tall = [(top, side) for top in range(0, tok_rows, TALL) for side in range(0, model_width, LANES)]
    for i, block_ref in enumerate(block_refs):
        for place, (top, side) in enumerate(tall):
            tile = block_ref[place * TALL : (place + 1) * TALL, :]
            base = i * tok_rows + top
            rows_ref[base : base + TALL, side : side + LANES] = tile
    rows = rows_ref[...]
    for start in range(0, hidden_width, TILE):
        cols = slice(start, start + TILE)
        gate = jnp.dot(rows, in_ref[0, 0, :, cols], preferred_element_type=jnp.float32)
        up = jnp.dot(rows, in_ref[0, 1, :, cols], preferred_element_type=jnp.float32)
        gate = gate * in_scale_ref[0, 0:1, cols].astype(jnp.float32)
        up = up * in_scale_ref[0, 1:2, cols].astype(jnp.float32)
        hidden_ref[:, cols] = (gate / (1.0 + jnp.exp(-gate)) * up).astype(jnp.bfloat16)
    experts = owners_ref.shape[1]
    lane = lax.broadcasted_iota(jnp.int32, owners_ref.shape, 1)
    here = owners_ref[...] == lax.axis_index("tok")
    mine = jnp.sum(jnp.where(here, lane, 0), axis=1, keepdims=True)
    label = lax.broadcasted_iota(jnp.int32, (2 * experts, tok_rows), 0)
    chosen = (label == mine) | (label == mine + experts)
    square = (tok_rows, tok_rows)
    same = lax.broadcasted_iota(jnp.int32, square, 0) == lax.broadcasted_iota(jnp.int32, square, 1)
    shares = []
    for block_ref in block_refs:
        table = block_ref[-2 * experts :, :].astype(jnp.float32)
        along = jnp.sum(jnp.where(chosen, table, 0.0), axis=0, keepdims=True)
        shares.append(jnp.sum(jnp.where(same, along, 0.0), axis=1, keepdims=True))
    hidden = hidden_ref[...]
    for start in range(0, model_width, TILE):
        cols = slice(start, start + TILE)
        out = jnp.dot(hidden, down_ref[0, :, cols], preferred_element_type=jnp.float32)
        out = out * down_scale_ref[:, cols].astype(jnp.float32)
        for i, (out_ref, share) in enumerate(zip(out_refs, shares)):
            weighted = out[i * tok_rows : (i + 1) * tok_rows] * share
            out_ref[:, cols] = weighted.astype(out_ref.dtype)


def visit(visitors, kinds, owners, in_q, in_scale, down_q, down_scale):
    hidden_width, model_width = down_q.shape[1:]
    tok_rows = (visitors[0].shape[0] - 2 * owners.shape[1]) * LANES // model_width
    count = len(visitors)
    operands = (owners, *visitors, in_q, in_scale, down_q, down_scale)
    return pl.pallas_call(
        functools.partial(visit_kernel, count),
        out_shape=tuple(jax.ShapeDtypeStruct((tok_rows, model_width), kind) for kind in kinds),
        in_specs=[pl.BlockSpec(memory_space=pltpu.VMEM)] * len(operands),
        out_specs=(pl.BlockSpec(memory_space=pltpu.VMEM),) * count,
        scratch_shapes=[
            pltpu.VMEM((count * tok_rows, model_width), jnp.bfloat16),
            pltpu.VMEM((count * tok_rows, hidden_width), jnp.bfloat16),
        ],
        compiler_params=pltpu.CompilerParams(vmem_limit_bytes=LARGE),
        cost_estimate=pl.CostEstimate(
            flops=2 * count * tok_rows * 3 * hidden_width * model_width,
            bytes_accessed=3 * count * tok_rows * model_width,
            transcendentals=0,
        ),
        name="visit",
    )(*operands)


def circulated(
    tokens, norm_gain, expert_ids, gate_weights, owner_map, in_q, in_scale, down_q, down_scale
):
    experts = owner_map.shape[0]
    devices = lax.axis_size("tok")
    ring, chips = ring_pairs(devices)
    swap = [(i, i ^ 1) for i in range(devices)]

    def moved(value, pairs):
        return lax.ppermute(value, "tok", pairs)

    raw = moved(tokens, ring)
    block, table = packed(tokens, norm_gain, expert_ids, gate_weights, experts)
    table = moved(table, ring)
    gain, owners, in_q, in_scale = loaded(norm_gain[None, :], owner_map[None, :], in_q, in_scale)
    down_q, down_scale = loaded(down_q, down_scale)
    blocks = (owners, in_q, in_scale, down_q, down_scale)
    back = moved(block, [(target, source) for source, target in ring])
    near = mended(raw, table, gain)
    parts = []
    for step in range(chips):
        here = {0: block, chips - 1: back}.get(step, near)
        other = moved(here, swap)
        if 0 < step < chips - 2:
            near = moved(near, ring)
        if step == chips - 2:
            (part,) = visit((here,), (jnp.float32,), *blocks)
            (lent,) = visit((other,), (jnp.bfloat16,), *blocks)
        else:
            part, lent = visit((here, other), (jnp.float32, jnp.bfloat16), *blocks)
        parts.append((part, moved(lent, swap)))

    def summed(step, rows, arrived):
        part, lent = (x[rows].astype(jnp.float32) for x in parts[step])
        return (part + lent + arrived.astype(jnp.float32)).astype(jnp.bfloat16)

    total = jnp.zeros((), jnp.bfloat16)
    for step in range(1, chips - 2):
        total = lax.ppermute(summed(step, slice(None), total), "tok", ring)
    shares = shares_of(tokens.shape[0])
    totals = {name: total[rows] for name, rows in shares.items()}
    for step in range(chips - 2, chips):
        for name, rows in shares.items():
            totals[name] = lax.ppermute(summed(step, rows, totals[name]), "tok", ring)
    out = []
    for name, rows in shares.items():
        out.append(summed(0, rows, totals[name]))
    return jnp.concatenate(out)


def shares_of(tok_rows):
    one, two = tok_rows // 16 * 7, tok_rows // 16 * 12
    return {"a": slice(0, one), "b": slice(one, two), "c": slice(two, tok_rows)}


def solution(mesh):
    devices = mesh.shape["tok"]
    row = P(("grp", "tok"), None)
    slot = [P("tok", *(None,) * extra) for extra in (3, 2, 2, 1)]

    def placed(body):
        return jax.shard_map(
            body,
            mesh=mesh,
            in_specs=(row, P(), row, row, P(), *slot),
            out_specs=row,
            check_vma=False,
        )

    def step(tokens, norm_gain, expert_ids, gate_weights, owner_map, *blocks):
        tok_rows = tokens.shape[0] // mesh.size
        experts = owner_map.shape[0]
        mean_load = tok_rows * expert_ids.shape[1] // experts
        routed = experts * (mean_load + mean_load // 2)
        arguments = (tokens, norm_gain, expert_ids, gate_weights, owner_map, *blocks)
        if tok_rows * devices > 2 * routed or devices < 16 or devices % 4 or tok_rows != LANES:
            return placed(exchanged)(*arguments)
        return placed(circulated)(*arguments)

    return step
```

```python
import functools

import jax
import jax.numpy as jnp
from jax import lax
from jax.experimental import pallas as pl
from jax.experimental.pallas import tpu as pltpu
from jax.sharding import PartitionSpec as P


LANES = 128
TALL = 16
TILE = 256
SMALL = 8 << 20
LARGE = 20 << 20


def expert_rows(batch_rows, in_blocks, in_scales, down_block, down_scales):
    gate_part = jnp.dot(batch_rows, in_blocks[0], preferred_element_type=jnp.float32) * in_scales[0]
    up_part = jnp.dot(batch_rows, in_blocks[1], preferred_element_type=jnp.float32) * in_scales[1]
    hidden = (jax.nn.silu(gate_part) * up_part).astype(jnp.bfloat16)
    return jnp.dot(hidden, down_block, preferred_element_type=jnp.float32) * down_scales


def normalized(tokens, norm_gain):
    values = tokens.astype(jnp.float32)
    row_scale = lax.rsqrt(jnp.mean(values * values, axis=1, keepdims=True) + 1e-06)
    return (values * row_scale * norm_gain).astype(jnp.bfloat16)


def exchanged(
    tokens, norm_gain, expert_ids, gate_weights, owner_map, in_q, in_scale, down_q, down_scale
):
    tok_rows, model_width = tokens.shape
    top_count = expert_ids.shape[1]
    experts = owner_map.shape[0]
    mean_load = tok_rows * top_count // experts
    capacity = mean_load + mean_load // 2
    normed = normalized(tokens, norm_gain)
    weights = gate_weights / jnp.sum(gate_weights, axis=1, keepdims=True)
    labels = jnp.arange(experts, dtype=jnp.int32)
    slot_table = jnp.sum(jnp.where(expert_ids[:, :, None] == labels, owner_map, 0), axis=2)
    flat_slot = slot_table.reshape(-1)
    onehot = (flat_slot[:, None] == labels).astype(jnp.int32)
    slot_rank = jnp.sum((jnp.cumsum(onehot, axis=0) - onehot) * onehot, axis=1)
    repeated = jnp.repeat(normed, top_count, axis=0)
    outgoing = (
        jnp.zeros((experts, capacity, model_width), jnp.bfloat16)
        .at[flat_slot, slot_rank]
        .set(repeated)
    )
    received = lax.all_to_all(outgoing, "tok", split_axis=0, concat_axis=0, tiled=True)
    source_count, slot_count, _ = received.shape
    flat_rows = received.reshape(source_count * slot_count, model_width)
    served = expert_rows(flat_rows, in_q[0], in_scale[0], down_q[0], down_scale[0])
    served = served.astype(jnp.bfloat16).reshape(source_count, slot_count, model_width)
    returned_rows = lax.all_to_all(served, "tok", split_axis=0, concat_axis=0, tiled=True)
    picked = returned_rows[flat_slot, slot_rank].reshape(tok_rows, top_count, model_width)
    mixed = jnp.sum(weights[:, :, None] * picked.astype(jnp.float32), axis=1)
    return mixed.astype(jnp.bfloat16)


def ring_pairs(devices):
    chips = devices // 2
    loop = list(range(0, chips, 2)) + list(range(chips - 1, 0, -2))
    pairs = []
    for place, chip in enumerate(loop):
        after = loop[(place + 1) % chips]
        pairs.append((2 * chip, 2 * after))
        pairs.append((2 * after + 1, 2 * chip + 1))
    return pairs, chips


def in_hbm(array):
    return pltpu.with_memory_space_constraint(array, pltpu.HBM)


def write_rows(tokens, gain, out_ref):
    tok_rows, model_width = tokens.shape
    for top in range(0, tok_rows, TALL):
        values = tokens[top : top + TALL, :].astype(jnp.float32)
        row_scale = lax.rsqrt(jnp.mean(values * values, axis=1, keepdims=True) + 1e-06)
        normed = (values * row_scale * gain[...]).astype(jnp.bfloat16)
        for side in range(0, model_width, LANES):
            row = top * model_width // LANES + side // LANES * TALL
            out_ref[row : row + TALL, :] = normed[:, side : side + LANES]


def packed_kernel(
    tokens_hbm, gain_hbm, ids_hbm, gates_hbm, out_ref, table_ref, tokens, gain, ids, gates, sems
):
    moves = [
        pltpu.make_async_copy(source, target, sems.at[i])
        for i, (source, target) in enumerate(
            ((ids_hbm, ids), (gates_hbm, gates), (tokens_hbm, tokens), (gain_hbm, gain))
        )
    ]
    for move in moves:
        move.start()
    moves[0].wait()
    moves[1].wait()
    weights = gates[...] / jnp.sum(gates[...], axis=0, keepdims=True)
    experts = table_ref.shape[0] // 2
    label = lax.broadcasted_iota(jnp.int32, (experts, tokens.shape[0]), 0)
    table = jnp.zeros(label.shape, jnp.float32)
    for k in range(ids.shape[0]):
        table += jnp.where(label == ids[k : k + 1, :], weights[k : k + 1, :], 0.0)
    high = table.astype(jnp.bfloat16)
    table_ref[:experts, :] = high
    table_ref[experts:, :] = (table - high.astype(jnp.float32)).astype(jnp.bfloat16)
    out_ref[-2 * experts :, :] = table_ref[...]
    moves[2].wait()
    moves[3].wait()
    write_rows(tokens, gain, out_ref)


def packed(tokens, norm_gain, expert_ids, gate_weights, experts):
    tok_rows, model_width = tokens.shape
    top_count = expert_ids.shape[1]
    size = tok_rows * model_width // LANES + 2 * experts
    return pl.pallas_call(
        packed_kernel,
        out_shape=tuple(
            jax.ShapeDtypeStruct((rows, LANES), jnp.bfloat16) for rows in (size, 2 * experts)
        ),
        in_specs=[pl.BlockSpec(memory_space=pltpu.HBM)] * 4,
        out_specs=(pl.BlockSpec(memory_space=pltpu.VMEM),) * 2,
        scratch_shapes=[
            pltpu.VMEM((tok_rows, model_width), jnp.bfloat16),
            pltpu.VMEM((1, model_width), jnp.float32),
            pltpu.VMEM((top_count, tok_rows), jnp.int32),
            pltpu.VMEM((top_count, tok_rows), jnp.float32),
            pltpu.SemaphoreType.DMA((4,)),
        ],
        compiler_params=pltpu.CompilerParams(vmem_limit_bytes=SMALL),
        name="packed",
    )(*map(in_hbm, (tokens, norm_gain[None, :], expert_ids.T, gate_weights.T)))


def mended_kernel(tokens_ref, table_ref, gain_ref, out_ref):
    out_ref[-table_ref.shape[0] :, :] = table_ref[...]
    write_rows(tokens_ref, gain_ref, out_ref)


def mended(tokens, table, gain):
    size = tokens.size // LANES + table.shape[0]
    return pl.pallas_call(
        mended_kernel,
        out_shape=jax.ShapeDtypeStruct((size, LANES), jnp.bfloat16),
        in_specs=[pl.BlockSpec(memory_space=pltpu.VMEM)] * 3,
        out_specs=pl.BlockSpec(memory_space=pltpu.VMEM),
        compiler_params=pltpu.CompilerParams(vmem_limit_bytes=SMALL),
        name="mended",
    )(tokens, table, gain)


def loaded_kernel(count, *refs):
    sources, targets, sems = refs[:count], refs[count : 2 * count], refs[-1]
    moves = [
        pltpu.make_async_copy(source, target, sems.at[i])
        for i, (source, target) in enumerate(zip(sources, targets))
    ]
    for move in moves:
        move.start()
    for move in moves:
        move.wait()


def loaded(*arrays):
    count = len(arrays)
    return pl.pallas_call(
        functools.partial(loaded_kernel, count),
        out_shape=tuple(jax.ShapeDtypeStruct(x.shape, x.dtype) for x in arrays),
        in_specs=[pl.BlockSpec(memory_space=pltpu.HBM)] * count,
        out_specs=(pl.BlockSpec(memory_space=pltpu.VMEM),) * count,
        scratch_shapes=[pltpu.SemaphoreType.DMA((count,))],
        compiler_params=pltpu.CompilerParams(vmem_limit_bytes=SMALL),
        cost_estimate=pl.CostEstimate(
            flops=0, bytes_accessed=2 * sum(x.size for x in arrays), transcendentals=0
        ),
        name="loaded",
    )(*map(in_hbm, arrays))


def visit_kernel(count, owners_ref, *refs):
    block_refs, refs = refs[:count], refs[count:]
    in_ref, in_scale_ref, down_ref, down_scale_ref = refs[:4]
    out_refs, (rows_ref, hidden_ref) = refs[4 : 4 + count], refs[4 + count :]
    tok_rows, model_width = out_refs[0].shape
    hidden_width = hidden_ref.shape[1]
    tall = [(top, side) for top in range(0, tok_rows, TALL) for side in range(0, model_width, LANES)]
    for i, block_ref in enumerate(block_refs):
        for place, (top, side) in enumerate(tall):
            tile = block_ref[place * TALL : (place + 1) * TALL, :]
            base = i * tok_rows + top
            rows_ref[base : base + TALL, side : side + LANES] = tile
    rows = rows_ref[...]
    for start in range(0, hidden_width, TILE):
        cols = slice(start, start + TILE)
        gate = jnp.dot(rows, in_ref[0, 0, :, cols], preferred_element_type=jnp.float32)
        up = jnp.dot(rows, in_ref[0, 1, :, cols], preferred_element_type=jnp.float32)
        gate = gate * in_scale_ref[0, 0:1, cols].astype(jnp.float32)
        up = up * in_scale_ref[0, 1:2, cols].astype(jnp.float32)
        hidden_ref[:, cols] = (gate / (1.0 + jnp.exp(-gate)) * up).astype(jnp.bfloat16)
    experts = owners_ref.shape[1]
    lane = lax.broadcasted_iota(jnp.int32, owners_ref.shape, 1)
    here = owners_ref[...] == lax.axis_index("tok")
    mine = jnp.sum(jnp.where(here, lane, 0), axis=1, keepdims=True)
    label = lax.broadcasted_iota(jnp.int32, (2 * experts, tok_rows), 0)
    chosen = (label == mine) | (label == mine + experts)
    square = (tok_rows, tok_rows)
    same = lax.broadcasted_iota(jnp.int32, square, 0) == lax.broadcasted_iota(jnp.int32, square, 1)
    shares = []
    for block_ref in block_refs:
        table = block_ref[-2 * experts :, :].astype(jnp.float32)
        along = jnp.sum(jnp.where(chosen, table, 0.0), axis=0, keepdims=True)
        shares.append(jnp.sum(jnp.where(same, along, 0.0), axis=1, keepdims=True))
    hidden = hidden_ref[...]
    for start in range(0, model_width, TILE):
        cols = slice(start, start + TILE)
        out = jnp.dot(hidden, down_ref[0, :, cols], preferred_element_type=jnp.float32)
        out = out * down_scale_ref[:, cols].astype(jnp.float32)
        for i, (out_ref, share) in enumerate(zip(out_refs, shares)):
            weighted = out[i * tok_rows : (i + 1) * tok_rows] * share
            out_ref[:, cols] = weighted.astype(out_ref.dtype)


def visit(visitors, kinds, owners, in_q, in_scale, down_q, down_scale):
    hidden_width, model_width = down_q.shape[1:]
    tok_rows = (visitors[0].shape[0] - 2 * owners.shape[1]) * LANES // model_width
    count = len(visitors)
    operands = (owners, *visitors, in_q, in_scale, down_q, down_scale)
    return pl.pallas_call(
        functools.partial(visit_kernel, count),
        out_shape=tuple(jax.ShapeDtypeStruct((tok_rows, model_width), kind) for kind in kinds),
        in_specs=[pl.BlockSpec(memory_space=pltpu.VMEM)] * len(operands),
        out_specs=(pl.BlockSpec(memory_space=pltpu.VMEM),) * count,
        scratch_shapes=[
            pltpu.VMEM((count * tok_rows, model_width), jnp.bfloat16),
            pltpu.VMEM((count * tok_rows, hidden_width), jnp.bfloat16),
        ],
        compiler_params=pltpu.CompilerParams(vmem_limit_bytes=LARGE),
        cost_estimate=pl.CostEstimate(
            flops=2 * count * tok_rows * 3 * hidden_width * model_width,
            bytes_accessed=3 * count * tok_rows * model_width,
            transcendentals=0,
        ),
        name="visit",
    )(*operands)


def finished_kernel(first, part_ref, lent_ref, arrived_ref, *refs):
    out_hbm, rows_ref, sem = refs[-3:]
    rows = slice(first, first + arrived_ref.shape[0])
    total = part_ref[rows, :] + lent_ref[rows, :].astype(jnp.float32)
    rows_ref[...] = (total + arrived_ref[...].astype(jnp.float32)).astype(jnp.bfloat16)
    move = pltpu.make_async_copy(rows_ref, out_hbm.at[rows, :], sem)
    move.start()
    move.wait()


def finished(out, part, lent, arrived, first):
    held = () if out is None else (out,)
    return pl.pallas_call(
        functools.partial(finished_kernel, first),
        out_shape=jax.ShapeDtypeStruct(part.shape, jnp.bfloat16),
        in_specs=[pl.BlockSpec(memory_space=pltpu.VMEM)] * 3
        + [pl.BlockSpec(memory_space=pltpu.HBM)] * len(held),
        out_specs=pl.BlockSpec(memory_space=pltpu.HBM),
        scratch_shapes=[pltpu.VMEM(arrived.shape, jnp.bfloat16), pltpu.SemaphoreType.DMA(())],
        input_output_aliases={3: 0} if held else {},
        compiler_params=pltpu.CompilerParams(vmem_limit_bytes=SMALL),
        name="finished",
    )(part, lent, arrived, *held)


def circulated(
    tokens, norm_gain, expert_ids, gate_weights, owner_map, in_q, in_scale, down_q, down_scale
):
    experts = owner_map.shape[0]
    devices = lax.axis_size("tok")
    ring, chips = ring_pairs(devices)
    swap = [(i, i ^ 1) for i in range(devices)]

    def moved(value, pairs):
        return lax.ppermute(value, "tok", pairs)

    raw = moved(tokens, ring)
    block, table = packed(tokens, norm_gain, expert_ids, gate_weights, experts)
    table = moved(table, ring)
    gain, owners, in_q, in_scale = loaded(norm_gain[None, :], owner_map[None, :], in_q, in_scale)
    down_q, down_scale = loaded(down_q, down_scale)
    blocks = (owners, in_q, in_scale, down_q, down_scale)
    back = moved(block, [(target, source) for source, target in ring])
    near = mended(raw, table, gain)
    parts = []
    for step in range(chips):
        here = {0: block, chips - 1: back}.get(step, near)
        other = moved(here, swap)
        if 0 < step < chips - 2:
            near = moved(near, ring)
        if step == chips - 2:
            (part,) = visit((here,), (jnp.float32,), *blocks)
            (lent,) = visit((other,), (jnp.bfloat16,), *blocks)
        else:
            part, lent = visit((here, other), (jnp.float32, jnp.bfloat16), *blocks)
        parts.append((part, moved(lent, swap)))

    def summed(step, rows, arrived):
        part, lent = (x[rows].astype(jnp.float32) for x in parts[step])
        return (part + lent + arrived.astype(jnp.float32)).astype(jnp.bfloat16)

    total = jnp.zeros((), jnp.bfloat16)
    for step in range(1, chips - 2):
        total = lax.ppermute(summed(step, slice(None), total), "tok", ring)
    shares = shares_of(tokens.shape[0])
    totals = {name: total[rows] for name, rows in shares.items()}
    for step in range(chips - 2, chips):
        for name, rows in shares.items():
            totals[name] = lax.ppermute(summed(step, rows, totals[name]), "tok", ring)
    out = None
    part, lent = parts[0]
    for name, rows in shares.items():
        out = finished(out, part, lent, totals[name], rows.start)
    return out


def shares_of(tok_rows):
    one, two = tok_rows // 16 * 7, tok_rows // 16 * 12
    return {"a": slice(0, one), "b": slice(one, two), "c": slice(two, tok_rows)}


def solution(mesh):
    devices = mesh.shape["tok"]
    row = P(("grp", "tok"), None)
    slot = [P("tok", *(None,) * extra) for extra in (3, 2, 2, 1)]

    def placed(body):
        return jax.shard_map(
            body,
            mesh=mesh,
            in_specs=(row, P(), row, row, P(), *slot),
            out_specs=row,
            check_vma=False,
        )

    def step(tokens, norm_gain, expert_ids, gate_weights, owner_map, *blocks):
        tok_rows = tokens.shape[0] // mesh.size
        experts = owner_map.shape[0]
        mean_load = tok_rows * expert_ids.shape[1] // experts
        routed = experts * (mean_load + mean_load // 2)
        arguments = (tokens, norm_gain, expert_ids, gate_weights, owner_map, *blocks)
        if tok_rows * devices > 2 * routed or devices < 16 or devices % 4 or tok_rows != LANES:
            return placed(exchanged)(*arguments)
        return placed(circulated)(*arguments)

    return step
```

```python
import functools

import jax
import jax.numpy as jnp
from jax import lax
from jax.experimental import pallas as pl
from jax.experimental.pallas import tpu as pltpu
from jax.sharding import PartitionSpec as P


LANES = 128
TALL = 16
TILE = 256
SMALL = 8 << 20
LARGE = 20 << 20


def expert_rows(batch_rows, in_blocks, in_scales, down_block, down_scales):
    gate_part = jnp.dot(batch_rows, in_blocks[0], preferred_element_type=jnp.float32) * in_scales[0]
    up_part = jnp.dot(batch_rows, in_blocks[1], preferred_element_type=jnp.float32) * in_scales[1]
    hidden = (jax.nn.silu(gate_part) * up_part).astype(jnp.bfloat16)
    return jnp.dot(hidden, down_block, preferred_element_type=jnp.float32) * down_scales


def normalized(tokens, norm_gain):
    values = tokens.astype(jnp.float32)
    row_scale = lax.rsqrt(jnp.mean(values * values, axis=1, keepdims=True) + 1e-06)
    return (values * row_scale * norm_gain).astype(jnp.bfloat16)


def exchanged(
    tokens, norm_gain, expert_ids, gate_weights, owner_map, in_q, in_scale, down_q, down_scale
):
    tok_rows, model_width = tokens.shape
    top_count = expert_ids.shape[1]
    experts = owner_map.shape[0]
    mean_load = tok_rows * top_count // experts
    capacity = mean_load + mean_load // 2
    normed = normalized(tokens, norm_gain)
    weights = gate_weights / jnp.sum(gate_weights, axis=1, keepdims=True)
    labels = jnp.arange(experts, dtype=jnp.int32)
    slot_table = jnp.sum(jnp.where(expert_ids[:, :, None] == labels, owner_map, 0), axis=2)
    flat_slot = slot_table.reshape(-1)
    onehot = (flat_slot[:, None] == labels).astype(jnp.int32)
    slot_rank = jnp.sum((jnp.cumsum(onehot, axis=0) - onehot) * onehot, axis=1)
    repeated = jnp.repeat(normed, top_count, axis=0)
    outgoing = (
        jnp.zeros((experts, capacity, model_width), jnp.bfloat16)
        .at[flat_slot, slot_rank]
        .set(repeated)
    )
    received = lax.all_to_all(outgoing, "tok", split_axis=0, concat_axis=0, tiled=True)
    source_count, slot_count, _ = received.shape
    flat_rows = received.reshape(source_count * slot_count, model_width)
    served = expert_rows(flat_rows, in_q[0], in_scale[0], down_q[0], down_scale[0])
    served = served.astype(jnp.bfloat16).reshape(source_count, slot_count, model_width)
    returned_rows = lax.all_to_all(served, "tok", split_axis=0, concat_axis=0, tiled=True)
    picked = returned_rows[flat_slot, slot_rank].reshape(tok_rows, top_count, model_width)
    mixed = jnp.sum(weights[:, :, None] * picked.astype(jnp.float32), axis=1)
    return mixed.astype(jnp.bfloat16)


def ring_pairs(devices):
    chips = devices // 2
    loop = list(range(0, chips, 2)) + list(range(chips - 1, 0, -2))
    pairs = []
    for place, chip in enumerate(loop):
        after = loop[(place + 1) % chips]
        pairs.append((2 * chip, 2 * after))
        pairs.append((2 * after + 1, 2 * chip + 1))
    return pairs, chips


def in_hbm(array):
    return pltpu.with_memory_space_constraint(array, pltpu.HBM)


def write_rows(tokens, gain, out_ref):
    tok_rows, model_width = tokens.shape
    for top in range(0, tok_rows, TALL):
        values = tokens[top : top + TALL, :].astype(jnp.float32)
        row_scale = lax.rsqrt(jnp.mean(values * values, axis=1, keepdims=True) + 1e-06)
        normed = (values * row_scale * gain[...]).astype(jnp.bfloat16)
        for side in range(0, model_width, LANES):
            row = top * model_width // LANES + side // LANES * TALL
            out_ref[row : row + TALL, :] = normed[:, side : side + LANES]


def packed_kernel(
    tokens_hbm, gain_hbm, ids_hbm, gates_hbm, out_ref, table_ref, tokens, gain, ids, gates, sems
):
    moves = [
        pltpu.make_async_copy(source, target, sems.at[i])
        for i, (source, target) in enumerate(
            ((ids_hbm, ids), (gates_hbm, gates), (tokens_hbm, tokens), (gain_hbm, gain))
        )
    ]
    for move in moves:
        move.start()
    moves[0].wait()
    moves[1].wait()
    weights = gates[...] / jnp.sum(gates[...], axis=0, keepdims=True)
    experts = table_ref.shape[0] // 2
    label = lax.broadcasted_iota(jnp.int32, (experts, tokens.shape[0]), 0)
    table = jnp.zeros(label.shape, jnp.float32)
    for k in range(ids.shape[0]):
        table += jnp.where(label == ids[k : k + 1, :], weights[k : k + 1, :], 0.0)
    high = table.astype(jnp.bfloat16)
    table_ref[:experts, :] = high
    table_ref[experts:, :] = (table - high.astype(jnp.float32)).astype(jnp.bfloat16)
    out_ref[-2 * experts :, :] = table_ref[...]
    moves[2].wait()
    moves[3].wait()
    write_rows(tokens, gain, out_ref)


def packed(tokens, norm_gain, expert_ids, gate_weights, experts):
    tok_rows, model_width = tokens.shape
    top_count = expert_ids.shape[1]
    size = tok_rows * model_width // LANES + 2 * experts
    return pl.pallas_call(
        packed_kernel,
        out_shape=tuple(
            jax.ShapeDtypeStruct((rows, LANES), jnp.bfloat16) for rows in (size, 2 * experts)
        ),
        in_specs=[pl.BlockSpec(memory_space=pltpu.HBM)] * 4,
        out_specs=(pl.BlockSpec(memory_space=pltpu.VMEM),) * 2,
        scratch_shapes=[
            pltpu.VMEM((tok_rows, model_width), jnp.bfloat16),
            pltpu.VMEM((1, model_width), jnp.float32),
            pltpu.VMEM((top_count, tok_rows), jnp.int32),
            pltpu.VMEM((top_count, tok_rows), jnp.float32),
            pltpu.SemaphoreType.DMA((4,)),
        ],
        compiler_params=pltpu.CompilerParams(vmem_limit_bytes=SMALL),
        name="packed",
    )(*map(in_hbm, (tokens, norm_gain[None, :], expert_ids.T, gate_weights.T)))


def mended_kernel(tokens_ref, table_ref, gain_ref, out_ref):
    out_ref[-table_ref.shape[0] :, :] = table_ref[...]
    write_rows(tokens_ref, gain_ref, out_ref)


def mended(tokens, table, gain):
    size = tokens.size // LANES + table.shape[0]
    return pl.pallas_call(
        mended_kernel,
        out_shape=jax.ShapeDtypeStruct((size, LANES), jnp.bfloat16),
        in_specs=[pl.BlockSpec(memory_space=pltpu.VMEM)] * 3,
        out_specs=pl.BlockSpec(memory_space=pltpu.VMEM),
        compiler_params=pltpu.CompilerParams(vmem_limit_bytes=SMALL),
        name="mended",
    )(tokens, table, gain)


def loaded_kernel(count, *refs):
    sources, targets, sems = refs[:count], refs[count : 2 * count], refs[-1]
    moves = [
        pltpu.make_async_copy(source, target, sems.at[i])
        for i, (source, target) in enumerate(zip(sources, targets))
    ]
    for move in moves:
        move.start()
    for move in moves:
        move.wait()


def loaded(*arrays):
    count = len(arrays)
    return pl.pallas_call(
        functools.partial(loaded_kernel, count),
        out_shape=tuple(jax.ShapeDtypeStruct(x.shape, x.dtype) for x in arrays),
        in_specs=[pl.BlockSpec(memory_space=pltpu.HBM)] * count,
        out_specs=(pl.BlockSpec(memory_space=pltpu.VMEM),) * count,
        scratch_shapes=[pltpu.SemaphoreType.DMA((count,))],
        compiler_params=pltpu.CompilerParams(vmem_limit_bytes=SMALL),
        cost_estimate=pl.CostEstimate(
            flops=0, bytes_accessed=2 * sum(x.size for x in arrays), transcendentals=0
        ),
        name="loaded",
    )(*map(in_hbm, arrays))


def visit_kernel(count, owners_ref, *refs):
    block_refs, refs = refs[:count], refs[count:]
    in_ref, in_scale_ref, down_ref, down_scale_ref = refs[:4]
    out_refs, (rows_ref, hidden_ref) = refs[4 : 4 + count], refs[4 + count :]
    tok_rows, model_width = out_refs[0].shape
    hidden_width = hidden_ref.shape[1]
    tall = [(top, side) for top in range(0, tok_rows, TALL) for side in range(0, model_width, LANES)]
    for i, block_ref in enumerate(block_refs):
        for place, (top, side) in enumerate(tall):
            tile = block_ref[place * TALL : (place + 1) * TALL, :]
            base = i * tok_rows + top
            rows_ref[base : base + TALL, side : side + LANES] = tile
    rows = rows_ref[...]
    for start in range(0, hidden_width, TILE):
        cols = slice(start, start + TILE)
        gate = jnp.dot(rows, in_ref[0, 0, :, cols], preferred_element_type=jnp.float32)
        up = jnp.dot(rows, in_ref[0, 1, :, cols], preferred_element_type=jnp.float32)
        gate = gate * in_scale_ref[0, 0:1, cols].astype(jnp.float32)
        up = up * in_scale_ref[0, 1:2, cols].astype(jnp.float32)
        hidden_ref[:, cols] = (gate / (1.0 + jnp.exp(-gate)) * up).astype(jnp.bfloat16)
    experts = owners_ref.shape[1]
    lane = lax.broadcasted_iota(jnp.int32, owners_ref.shape, 1)
    here = owners_ref[...] == lax.axis_index("tok")
    mine = jnp.sum(jnp.where(here, lane, 0), axis=1, keepdims=True)
    label = lax.broadcasted_iota(jnp.int32, (2 * experts, tok_rows), 0)
    chosen = (label == mine) | (label == mine + experts)
    square = (tok_rows, tok_rows)
    same = lax.broadcasted_iota(jnp.int32, square, 0) == lax.broadcasted_iota(jnp.int32, square, 1)
    shares = []
    for block_ref in block_refs:
        table = block_ref[-2 * experts :, :].astype(jnp.float32)
        along = jnp.sum(jnp.where(chosen, table, 0.0), axis=0, keepdims=True)
        shares.append(jnp.sum(jnp.where(same, along, 0.0), axis=1, keepdims=True))
    hidden = hidden_ref[...]
    for start in range(0, model_width, TILE):
        cols = slice(start, start + TILE)
        out = jnp.dot(hidden, down_ref[0, :, cols], preferred_element_type=jnp.float32)
        out = out * down_scale_ref[:, cols].astype(jnp.float32)
        for i, (out_ref, share) in enumerate(zip(out_refs, shares)):
            weighted = out[i * tok_rows : (i + 1) * tok_rows] * share
            out_ref[:, cols] = weighted.astype(out_ref.dtype)


def visit(visitors, kinds, owners, in_q, in_scale, down_q, down_scale):
    hidden_width, model_width = down_q.shape[1:]
    tok_rows = (visitors[0].shape[0] - 2 * owners.shape[1]) * LANES // model_width
    count = len(visitors)
    operands = (owners, *visitors, in_q, in_scale, down_q, down_scale)
    return pl.pallas_call(
        functools.partial(visit_kernel, count),
        out_shape=tuple(jax.ShapeDtypeStruct((tok_rows, model_width), kind) for kind in kinds),
        in_specs=[pl.BlockSpec(memory_space=pltpu.VMEM)] * len(operands),
        out_specs=(pl.BlockSpec(memory_space=pltpu.VMEM),) * count,
        scratch_shapes=[
            pltpu.VMEM((count * tok_rows, model_width), jnp.bfloat16),
            pltpu.VMEM((count * tok_rows, hidden_width), jnp.bfloat16),
        ],
        compiler_params=pltpu.CompilerParams(vmem_limit_bytes=LARGE),
        cost_estimate=pl.CostEstimate(
            flops=2 * count * tok_rows * 3 * hidden_width * model_width,
            bytes_accessed=3 * count * tok_rows * model_width,
            transcendentals=0,
        ),
        name="visit",
    )(*operands)


def added_kernel(rows, part_ref, lent_ref, arrived_ref, out_ref):
    total = part_ref[rows, :] + lent_ref[rows, :].astype(jnp.float32)
    out_ref[...] = (total + arrived_ref[...].astype(jnp.float32)).astype(jnp.bfloat16)


def finished_kernel(first, part_ref, lent_ref, arrived_ref, *refs):
    out_hbm, rows_ref, sem = refs[-3:]
    rows = slice(first, first + arrived_ref.shape[0])
    total = part_ref[rows, :] + lent_ref[rows, :].astype(jnp.float32)
    rows_ref[...] = (total + arrived_ref[...].astype(jnp.float32)).astype(jnp.bfloat16)
    move = pltpu.make_async_copy(rows_ref, out_hbm.at[rows, :], sem)
    move.start()
    move.wait()


def finished(out, part, lent, arrived, first):
    held = () if out is None else (out,)
    return pl.pallas_call(
        functools.partial(finished_kernel, first),
        out_shape=jax.ShapeDtypeStruct(part.shape, jnp.bfloat16),
        in_specs=[pl.BlockSpec(memory_space=pltpu.VMEM)] * 3
        + [pl.BlockSpec(memory_space=pltpu.HBM)] * len(held),
        out_specs=pl.BlockSpec(memory_space=pltpu.HBM),
        scratch_shapes=[pltpu.VMEM(arrived.shape, jnp.bfloat16), pltpu.SemaphoreType.DMA(())],
        input_output_aliases={3: 0} if held else {},
        compiler_params=pltpu.CompilerParams(vmem_limit_bytes=SMALL),
        name="finished",
    )(part, lent, arrived, *held)


def circulated(
    tokens, norm_gain, expert_ids, gate_weights, owner_map, in_q, in_scale, down_q, down_scale
):
    experts = owner_map.shape[0]
    devices = lax.axis_size("tok")
    ring, chips = ring_pairs(devices)
    swap = [(i, i ^ 1) for i in range(devices)]

    def moved(value, pairs):
        return lax.ppermute(value, "tok", pairs)

    raw = moved(tokens, ring)
    block, table = packed(tokens, norm_gain, expert_ids, gate_weights, experts)
    table = moved(table, ring)
    gain, owners, in_q, in_scale = loaded(norm_gain[None, :], owner_map[None, :], in_q, in_scale)
    down_q, down_scale = loaded(down_q, down_scale)
    blocks = (owners, in_q, in_scale, down_q, down_scale)
    back = moved(block, [(target, source) for source, target in ring])
    near = mended(raw, table, gain)
    parts = []
    for step in range(chips):
        here = {0: block, chips - 1: back}.get(step, near)
        other = moved(here, swap)
        if 0 < step < chips - 2:
            near = moved(near, ring)
        if step == chips - 2:
            (part,) = visit((here,), (jnp.float32,), *blocks)
            (lent,) = visit((other,), (jnp.bfloat16,), *blocks)
        else:
            part, lent = visit((here, other), (jnp.float32, jnp.bfloat16), *blocks)
        parts.append((part, moved(lent, swap)))

    def summed(step, rows, arrived):
        part, lent = (x[rows].astype(jnp.float32) for x in parts[step])
        return (part + lent + arrived.astype(jnp.float32)).astype(jnp.bfloat16)

    def added(step, rows, arrived):
        return pl.pallas_call(
            functools.partial(added_kernel, rows),
            out_shape=jax.ShapeDtypeStruct(arrived.shape, jnp.bfloat16),
            in_specs=[pl.BlockSpec(memory_space=pltpu.VMEM)] * 3,
            out_specs=pl.BlockSpec(memory_space=pltpu.VMEM),
            compiler_params=pltpu.CompilerParams(vmem_limit_bytes=SMALL),
            name="added",
        )(*parts[step], arrived)

    total = jnp.zeros((), jnp.bfloat16)
    for step in range(1, chips - 2):
        total = lax.ppermute(summed(step, slice(None), total), "tok", ring)
    shares = shares_of(tokens.shape[0])
    totals = {name: total[rows] for name, rows in shares.items()}
    for step in range(chips - 2, chips):
        for name, rows in shares.items():
            add = summed if step < chips - 1 else added
            totals[name] = lax.ppermute(add(step, rows, totals[name]), "tok", ring)
    out = None
    part, lent = parts[0]
    for name, rows in shares.items():
        out = finished(out, part, lent, totals[name], rows.start)
    return out


def shares_of(tok_rows):
    one, two = tok_rows // 16 * 6, tok_rows // 16 * 11
    return {"a": slice(0, one), "b": slice(one, two), "c": slice(two, tok_rows)}


def solution(mesh):
    devices = mesh.shape["tok"]
    row = P(("grp", "tok"), None)
    slot = [P("tok", *(None,) * extra) for extra in (3, 2, 2, 1)]

    def placed(body):
        return jax.shard_map(
            body,
            mesh=mesh,
            in_specs=(row, P(), row, row, P(), *slot),
            out_specs=row,
            check_vma=False,
        )

    def step(tokens, norm_gain, expert_ids, gate_weights, owner_map, *blocks):
        tok_rows = tokens.shape[0] // mesh.size
        experts = owner_map.shape[0]
        mean_load = tok_rows * expert_ids.shape[1] // experts
        routed = experts * (mean_load + mean_load // 2)
        arguments = (tokens, norm_gain, expert_ids, gate_weights, owner_map, *blocks)
        if tok_rows * devices > 2 * routed or devices < 16 or devices % 4 or tok_rows != LANES:
            return placed(exchanged)(*arguments)
        return placed(circulated)(*arguments)

    return step
```
